768 devices in a mesh: curve: 96 (over z, y), slab: 8 (over x, core).
Axes of the slice: x: 4, y: 8, z: 12, core: 2. Of those that a mesh axis runs over, the one named last changes fastest.
Arguments:
- state: float32 [5, 125, 8, 12288], P(None, None, 'slab', 'curve'), as said below
- levels: int32 [8, 12288], P('slab', 'curve'), may hold values from 0 to 2
- neighbours: int32 [6, 8, 12288], P(None, 'slab', 'curve'), may hold values from 0 to 98303, as said below
- shifts: int32 [8, 96], P('slab', 'curve'), may hold values from -32 to 32
Outputs:
- moved: float32 [5, 125, 8, 12288], P(None, None, 'slab', 'curve')
- mortar: float32 [5, 25, 8, 12288], P(None, None, 'slab', 'curve')
The draws below stay inside these ranges and needn't reach their ends.
Inputs may be any that keep to these rules, and one draw needn't show every extreme that they name: `neighbours`: faces 0 and 1 name an element of the row before and the row after (cyclically), faces 2 and 3 one of the same row; for faces 0 to 3 the named element sits in the same block of 128 positions; face 4 names one of the same row in the same block or the block before, face 5 in the same block or the block after (cyclically over blocks). `state`: density and pressure positive.
All inputs are finite; a program needn't handle non-finite values.
Results may differ from the reference program's by a relative error of at most 0.00021.
Values sent between devices are 32-bit elements; how exact they have to be, the bound alone decides.
No kernel may reach another device: no remote copies, remote signals or barrier semaphores. Data moves between devices by JAX's collectives and lax.ppermute only.
A program may use at most 32 MiB of HBM per device.

```python
import jax
import jax.numpy as jnp
import numpy as np
from jax import lax

NV = 5
ORDER = 5
NODES = 125
FACE = 25
EL = 128
SHIFT_MAX = 32
ROWS = 8
BLOCKS = 96
ECURVE = 12288


GAMMA = 1.4


def draw_state(key, part):
    keys = jax.random.split(jax.random.fold_in(key, 11), 6)
    shape = (NODES, ROWS, ECURVE)
    density = jax.random.uniform(keys[1], shape, jnp.float32, 0.6, 1.6)
    velocity = 0.4 * jax.random.normal(keys[2], (3,) + shape, jnp.float32)
    press = jax.random.uniform(keys[4], shape, jnp.float32, 0.6, 1.6)
    momentum = density * velocity
    energy = press / (GAMMA - 1.0) + 0.5 * density * jnp.sum(velocity * velocity, axis=0)
    return jnp.concatenate([density[None], momentum, energy[None]], axis=0).astype(jnp.float32)


def draw_neighbours(key, part):
    keys = jax.random.split(jax.random.fold_in(key, 23), 2)
    offsets = jax.random.randint(keys[0], (6, ROWS, ECURVE), 0, EL)
    steps = jax.random.randint(keys[1], (2, ROWS, ECURVE), 0, 2)
    rows = jnp.arange(ROWS, dtype=jnp.int32)[:, None] + jnp.zeros((ROWS, ECURVE), jnp.int32)
    block = jnp.arange(ECURVE, dtype=jnp.int32)[None, :] // EL + jnp.zeros((ROWS, ECURVE), jnp.int32)
    row_of = [(rows - 1) % ROWS, (rows + 1) % ROWS, rows, rows, rows, rows]
    block_of = [block, block, block, block, (block - steps[0]) % BLOCKS, (block + steps[1]) % BLOCKS]
    lists = [row_of[f] * ECURVE + block_of[f] * EL + offsets[f] for f in range(6)]
    return jnp.stack(lists).astype(jnp.int32)


def draw_shifts(key, part):
    keys = jax.random.split(jax.random.fold_in(key, 37), 2)
    values = jax.random.randint(keys[0], (ROWS * BLOCKS,), -SHIFT_MAX, SHIFT_MAX + 1)
    chosen = jax.random.permutation(keys[1], ROWS * BLOCKS)
    values = values.at[chosen[0]].set(SHIFT_MAX).at[chosen[1]].set(-SHIFT_MAX)
    return values.reshape(ROWS, BLOCKS).astype(jnp.int32)


def with_ends(values, key, low, high):
    longest = values.shape.index(max(values.shape))
    spots = []
    for shift in (0, 1):
        where = [jax.random.randint(jax.random.fold_in(key, axis), (), 0, length) for axis, length in enumerate(values.shape)]
        where[longest] = (where[longest] + shift) % values.shape[longest]
        spots.append(tuple(where))
    return values.at[spots[0]].set(low).at[spots[1]].set(high)


def setup_inputs(seed: int = 0) -> dict:
    splits = jax.random.split(jax.random.key(seed), 5)
    state = draw_state(jax.random.fold_in(splits[4], 71), 0)
    levels = with_ends(jax.random.randint(splits[1], (ROWS, ECURVE), 0, 3), jax.random.fold_in(splits[1], 1), 0, 2).astype(jnp.int32)
    neighbours = draw_neighbours(jax.random.fold_in(splits[4], 71), 0)
    shifts = draw_shifts(jax.random.fold_in(splits[4], 71), 0)
    return {"state": state, "levels": levels, "neighbours": neighbours, "shifts": shifts}


GAMMA = 1.4
CFL = 0.05
END_WEIGHT = 0.1

def derivative_matrix():
    points = np.array([-1.0, -np.sqrt(3.0 / 7.0), 0.0, np.sqrt(3.0 / 7.0), 1.0])
    bary = np.array([1.0 / np.prod([points[j] - points[k] for k in range(5) if k != j]) for j in range(5)])
    table = np.zeros((5, 5))
    for i in range(5):
        for j in range(5):
            if i != j:
                table[i, j] = bary[j] / bary[i] / (points[i] - points[j])
        table[i, i] = -np.sum(table[i])
    return jnp.asarray(table, jnp.float32)

def euler_flux(u, d):
    density = u[0]
    momentum = u[1:4]
    energy = u[4]
    velocity = momentum / density
    press = (GAMMA - 1.0) * (energy - 0.5 * lax.optimization_barrier(jnp.sum(momentum * velocity, axis=0)))
    along = velocity[d]
    parts = [momentum[d]]
    for a in range(3):
        term = momentum[a] * along
        if a == d:
            term = term + press
        parts.append(term)
    parts.append((energy + press) * along)
    return jnp.stack(parts)

def wave_speed(u):
    velocity = u[1:4] / u[0]
    press = (GAMMA - 1.0) * (u[4] - 0.5 * lax.optimization_barrier(jnp.sum(u[1:4] * velocity, axis=0)))
    return jnp.sqrt(lax.optimization_barrier(jnp.sum(velocity * velocity, axis=0))) + jnp.sqrt(GAMMA * press / u[0])

def rusanov(lower, upper, d, lam):
    return 0.5 * (euler_flux(lower, d) + euler_flux(upper, d)) - 0.5 * lam * (upper - lower)

def own_faces(u5):
    return [u5[:, :, :, 0], u5[:, :, :, 4], u5[:, :, 0], u5[:, :, 4], u5[:, 0], u5[:, 4]]

def onehot(axis, index):
    shape = [1, 1, 1, 1, 1]
    shape[axis] = 5
    return (jnp.arange(5) == index).astype(jnp.float32).reshape(shape)

def residual(u5, outer, scale, lam):
    table = derivative_matrix()
    high = lax.Precision.HIGHEST
    div = jnp.einsum('ai,vkjie->vkjae', table, euler_flux(u5, 0), precision=high)
    div = div + jnp.einsum('aj,vkjie->vkaie', table, euler_flux(u5, 1), precision=high)
    div = div + jnp.einsum('ak,vkjie->vajie', table, euler_flux(u5, 2), precision=high)
    faces = own_faces(u5)
    correct = jnp.zeros_like(u5)
    for d in range(3):
        axis = 3 - d
        inner_low = faces[2 * d]
        inner_high = faces[2 * d + 1]
        lift_low = (rusanov(outer[2 * d], inner_low, d, lam) - euler_flux(inner_low, d)) / END_WEIGHT
        lift_high = (rusanov(inner_high, outer[2 * d + 1], d, lam) - euler_flux(inner_high, d)) / END_WEIGHT
        correct = correct + jnp.expand_dims(lift_low, axis) * onehot(axis, 0)
        correct = correct - jnp.expand_dims(lift_high, axis) * onehot(axis, 4)
    return scale * (correct - div)

def reference(state, levels, neighbours, shifts):
    total = ROWS * ECURVE
    u5 = state.reshape(NV, ORDER, ORDER, ORDER, total)
    scale = jnp.exp2(levels.reshape(total).astype(jnp.float32))
    speed = wave_speed(u5)
    lam = jnp.max(speed)
    top = jnp.max(speed * scale)
    faces = own_faces(u5)
    outer = []
    for f in range(6):
        opposite = faces[f + 1 - 2 * (f % 2)]
        outer.append(jnp.take(opposite, neighbours[f].reshape(total), axis=-1))
    new = u5 + CFL / top * residual(u5, outer, scale, lam)
    rowwise = new.reshape(NV, ORDER, ORDER, ORDER, ROWS, ECURVE)
    upper = rowwise[:, 4]
    before = jnp.roll(upper, 1, axis=-1)
    mflux = rusanov(before, rowwise[:, 0], 2, lam)
    position = jnp.arange(ECURVE, dtype=jnp.int32)
    block = position // EL
    source = (position[None, :] + shifts[:, block]) % ECURVE
    flat = (jnp.arange(ROWS, dtype=jnp.int32)[:, None] * ECURVE + source).astype(jnp.int32).reshape(-1)
    moved = jnp.take(new.reshape(NV * NODES, total), flat, axis=1).reshape(NV, NODES, ROWS, ECURVE)
    mortar = jnp.take(mflux.reshape(NV * FACE, total), flat, axis=1).reshape(NV, FACE, ROWS, ECURVE)
    return (moved, mortar)
```

```python
import jax
import jax.numpy as jnp
import numpy as np
from jax import lax
from jax.experimental import pallas as pl
from jax.experimental.pallas import tpu as pltpu
from jax.sharding import PartitionSpec as P

NV = 5
NODES = 125
FACE = 25
EL = 128
GAMMA = 1.4
CFL = 0.05
END_WEIGHT = 0.1
PAD = 128
FPAD = 32
LANES = 42
Z, Y, X, CORES = 12, 8, 4, 2
HIGH = lax.Precision.HIGHEST
AXES = ("curve", "slab")


def flat(z, y, x, core):
    return (z * Y + y) * X * CORES + x * CORES + core


def plane_groups():
    return [
        [flat(z, y, x, c) for y in range(Y) for x in range(X)] for z in range(Z) for c in range(CORES)
    ]


def column_groups():
    return [
        [flat(z, y, x, c) for z in range(Z) for c in range(CORES)] for y in range(Y) for x in range(X)
    ]


def derivative_matrix():
    points = np.array([-1.0, -np.sqrt(3.0 / 7.0), 0.0, np.sqrt(3.0 / 7.0), 1.0])
    bary = np.array(
        [1.0 / np.prod([points[j] - points[k] for k in range(5) if k != j]) for j in range(5)]
    )
    table = np.zeros((5, 5))
    for i in range(5):
        for j in range(5):
            if i != j:
                table[i, j] = bary[j] / bary[i] / (points[i] - points[j])
        table[i, i] = -np.sum(table[i])
    return table


def face_nodes(f):
    d, end = f // 2, 4 * (f % 2)
    nodes = []
    for b in range(5):
        for a in range(5):
            ijk = {0: (end, a, b), 1: (a, end, b), 2: (a, b, end)}[d]
            nodes.append(ijk[0] + 5 * ijk[1] + 25 * ijk[2])
    return nodes


def operator_table():
    half = 0.5 / END_WEIGHT
    table = derivative_matrix()
    eye = np.eye(5)
    volume = np.zeros((PAD, 3 * PAD))
    for d, parts in enumerate(((eye, eye, table), (eye, table, eye), (table, eye, eye))):
        full = np.kron(parts[0], np.kron(parts[1], parts[2]))
        volume[:NODES, d * PAD : d * PAD + NODES] = -full
    place = np.zeros((PAD, 6 * FPAD))
    count = np.zeros((PAD, 1))
    for f in range(6):
        sign = 1.0 - 2.0 * (f % 2)
        for m, n in enumerate(face_nodes(f)):
            place[n, f * FPAD + m] = 1.0
            volume[n, (f // 2) * PAD + n] -= sign * half
            count[n, 0] += half
    return np.concatenate([volume, place, np.broadcast_to(count, (PAD, EL))], axis=1).astype(np.float32)


def flux(u, d):
    density, momentum, energy = u[0], u[1:4], u[4]
    inverse = 1.0 / density
    velocity = [m * inverse for m in momentum]
    kinetic = momentum[0] * velocity[0] + momentum[1] * velocity[1] + momentum[2] * velocity[2]
    press = (GAMMA - 1.0) * (energy - 0.5 * kinetic)
    along = velocity[d]
    parts = [momentum[d]]
    for a in range(3):
        term = momentum[a] * along
        parts.append(term + press if a == d else term)
    parts.append((energy + press) * along)
    return parts


def all_fluxes(u):
    density, momentum, energy = u[0], u[1:4], u[4]
    inverse = 1.0 / density
    velocity = [m * inverse for m in momentum]
    kinetic = momentum[0] * velocity[0] + momentum[1] * velocity[1] + momentum[2] * velocity[2]
    press = (GAMMA - 1.0) * (energy - 0.5 * kinetic)
    total = energy + press
    out = []
    for d in range(3):
        along = velocity[d]
        parts = [momentum[d]]
        for a in range(3):
            term = momentum[a] * along
            parts.append(term + press if a == d else term)
        parts.append(total * along)
        out.append(parts)
    return out


def lane_pair(lam, top):
    lane = lax.broadcasted_iota(jnp.int32, (1, EL), 1)
    return jnp.where(lane < EL // 2, lam, top)


def start_kernel(state, levels, u, scale_row, peak, xlo, xhi, zlo, zhi, level, sem):
    copies = [
        pltpu.make_async_copy(state.at[v, :, 0], u.at[v, pl.ds(0, NODES)], sem.at[v]) for v in range(NV)
    ]
    copies.append(pltpu.make_async_copy(levels, level, sem.at[NV]))
    for copy in copies:
        copy.start()
    for v in range(NV):
        u[v, NODES:PAD, :] = jnp.full((PAD - NODES, EL), 1.0 if v == 0 else 0.0, jnp.float32)
    for copy in copies:
        copy.wait()
    scale = jnp.exp2(level[...].astype(jnp.float32))
    scale_row[...] = scale
    density, energy = u[0], u[4]
    momentum = [u[1], u[2], u[3]]
    inverse = 1.0 / density
    velocity = [m * inverse for m in momentum]
    kinetic = momentum[0] * velocity[0] + momentum[1] * velocity[1] + momentum[2] * velocity[2]
    press = (GAMMA - 1.0) * (energy - 0.5 * kinetic)
    square = velocity[0] * velocity[0] + velocity[1] * velocity[1] + velocity[2] * velocity[2]
    speed = jnp.sqrt(square) + jnp.sqrt(GAMMA * press * inverse)
    speed = jnp.max(speed, axis=0, keepdims=True)
    lam = jnp.max(speed, axis=1, keepdims=True)
    top = jnp.max(speed * scale, axis=1, keepdims=True)
    peak[...] = jnp.broadcast_to(lane_pair(lam, top)[None], peak.shape)
    ones = jnp.full((FPAD - FACE, EL), 1.0, jnp.float32)
    for v in range(NV):
        row = v * FPAD
        xlo[row : row + FACE, :] = u[v, pl.ds(0, FACE, stride=5), :]
        xhi[row : row + FACE, :] = u[v, pl.ds(4, FACE, stride=5), :]
        zlo[row : row + FACE, :] = u[v, 0:FACE, :]
        zhi[row : row + FACE, :] = u[v, NODES - FACE : NODES, :]
        for ref in (xlo, xhi, zlo, zhi):
            ref[row + FACE : row + FPAD, :] = ones


def dot(a, b):
    return jnp.dot(a, b, precision=HIGH, preferred_element_type=jnp.float32)


def middle_kernel(
    u, xlo, xhi, zlo, zhi, xbelow, xabove, zbelow, zabove, neighbours, scale_row, peaks, operator,
    a_out, b_out, to_left, to_right, peak, ylo, yhi, rhs, outer,
):
    best = jnp.max(peaks[...], axis=0)
    peak[...] = jnp.broadcast_to(best[None], peak.shape)
    scale = scale_row[...]
    ones = jnp.full((FPAD - FACE, EL), 1.0, jnp.float32)
    for v in range(NV):
        row = v * FPAD
        for k in range(5):
            ylo[row + 5 * k : row + 5 * k + 5, :] = u[v, 25 * k : 25 * k + 5, :]
            yhi[row + 5 * k : row + 5 * k + 5, :] = u[v, 25 * k + 20 : 25 * k + 25, :]
        ylo[row + FACE : row + FPAD, :] = ones
        yhi[row + FACE : row + FPAD, :] = ones
    for d, parts in enumerate(all_fluxes([u[v] for v in range(NV)])):
        for v in range(NV):
            rhs[d * PAD : (d + 1) * PAD, v * EL : (v + 1) * EL] = parts[v]
    source = lax.broadcasted_iota(jnp.int32, (EL, EL), 0)
    named = [neighbours[f] for f in range(6)]
    home = named[2] >> 7
    half = 0.5 / END_WEIGHT
    for f in range(6):
        offset = named[f] & (EL - 1)
        if f < 4:
            trace = (xbelow, xabove, yhi, ylo)[f]
            got = dot(trace[...], (source == offset).astype(jnp.float32))
        else:
            here = (named[f] >> 7) == home
            mine, other = ((zhi, zbelow), (zlo, zabove))[f - 4]
            own_index = jnp.where(here, offset, -1)
            other_index = jnp.where(here, -1, offset)
            got = dot(mine[...], (source == own_index).astype(jnp.float32)) + dot(
                other[...], (source == other_index).astype(jnp.float32)
            )
        got = [got[v * FPAD : (v + 1) * FPAD] for v in range(NV)]
        sign = half * (1.0 - 2.0 * (f % 2))
        parts = flux(got, f // 2)
        for v in range(NV):
            rhs[3 * PAD + f * FPAD : 3 * PAD + (f + 1) * FPAD, v * EL : (v + 1) * EL] = sign * parts[v]
            outer[f * FPAD : (f + 1) * FPAD, v * EL : (v + 1) * EL] = half * got[v]
    place = 3 * PAD + 6 * FPAD
    a = dot(operator[:, :place], rhs[...])
    b = dot(operator[:, 3 * PAD : place], outer[...])
    count = operator[:, place:]
    lane = lax.broadcasted_iota(jnp.int32, (PAD, EL), 1)
    for v in range(NV):
        uv = u[v]
        av = a[:, v * EL : (v + 1) * EL] * scale
        bv = (b[:, v * EL : (v + 1) * EL] - count * uv) * scale
        a_out[v] = av
        b_out[v] = bv
        to_left[v] = jnp.where(
            lane < LANES,
            uv,
            jnp.where(lane < 2 * LANES, pltpu.roll(av, LANES, 1), pltpu.roll(bv, 2 * LANES, 1)),
        )
        to_right[v] = jnp.where(
            lane < LANES,
            pltpu.roll(uv, LANES, 1),
            jnp.where(lane < 2 * LANES, pltpu.roll(av, 2 * LANES, 1), pltpu.roll(bv, 3 * LANES, 1)),
        )


def last_kernel(shifts, u, a, b, from_left, from_right, peaks, moved, mortar, new, surface, sem):
    best = jnp.max(peaks[...], axis=0)
    lam = jnp.max(best[:, : EL // 2], axis=1, keepdims=True)
    top = jnp.max(best[:, EL // 2 :], axis=1, keepdims=True)
    step = CFL / top
    shift = shifts[0, 0]
    ahead = shift >= 1
    turn = jnp.where(ahead, 2 * EL - shift, 2 * EL - shift - LANES) % EL
    own_turn = (2 * EL - shift) % EL
    lane = lax.broadcasted_iota(jnp.int32, (PAD, EL), 1)
    first = jnp.where(ahead, EL - shift, 0)
    end = jnp.where(ahead, EL, -shift)
    outside = (lane >= first) & (lane < end)
    lane_up = lax.broadcasted_iota(jnp.int32, (FPAD, EL), 1)
    outside_up = (lane_up >= jnp.where(ahead, first + 1, 0)) & (lane_up < end + 1)
    low, high = [], []
    copies = []
    for v in range(NV):
        own = u[v] + step * (a[v] + lam * b[v])
        pack = jnp.where(ahead, from_right[v], from_left[v])
        halo = pack + step * (pltpu.roll(pack, EL - LANES, 1) + lam * pltpu.roll(pack, EL - 2 * LANES, 1))
        own = pltpu.roll(own, own_turn, 1)
        halo = pltpu.roll(halo, turn, 1)
        block = jnp.where(outside, halo, own)
        new[v] = block
        copy = pltpu.make_async_copy(new.at[v, pl.ds(0, NODES)], moved.at[v, :, 0], sem.at[v])
        copy.start()
        copies.append(copy)
        low.append(block[:FPAD])
        before = jnp.where(
            outside_up, pltpu.roll(halo[PAD - FPAD :], 1, 1), pltpu.roll(own[PAD - FPAD :], 1, 1)
        )
        high.append(pltpu.roll(before, FPAD - 4, 0))
    lower, upper = flux(high, 2), flux(low, 2)
    for v in range(NV):
        surface[v] = 0.5 * (lower[v] + upper[v]) - 0.5 * lam * (low[v] - high[v])
        copy = pltpu.make_async_copy(
            surface.at[v, pl.ds(0, FACE)], mortar.at[v, :, 0], sem.at[NV + v]
        )
        copy.start()
        copies.append(copy)
    for copy in copies:
        copy.wait()


def shape(*dims):
    return jax.ShapeDtypeStruct(dims, jnp.float32)


VMEM = pl.BlockSpec(memory_space=pltpu.VMEM)
ANY = pl.BlockSpec(memory_space=pl.ANY)
HBM = pl.BlockSpec(memory_space=pltpu.HBM)
SMEM = pl.BlockSpec(memory_space=pltpu.SMEM)


def shifted(value, axis, step):
    count = lax.axis_size(axis)
    return lax.ppermute(value, axis, [(i, (i + step) % count) for i in range(count)])


def exchanged(value, groups):
    return lax.all_to_all(value, AXES, 0, 0, tiled=True, axis_index_groups=groups)


def on_device(state, levels, neighbours, shifts):
    planes, columns = plane_groups(), column_groups()
    operator = jnp.asarray(operator_table())
    trace = shape(NV * FPAD, EL)
    block = shape(NV, PAD, EL)
    u, scale, peak, xlo, xhi, zlo, zhi = pl.pallas_call(
        start_kernel,
        out_shape=(block, shape(1, EL), shape(len(planes[0]), 1, EL), trace, trace, trace, trace),
        in_specs=[HBM, HBM],
        out_specs=(VMEM,) * 7,
        scratch_shapes=[pltpu.VMEM((1, EL), jnp.int32), pltpu.SemaphoreType.DMA((NV + 1,))],
        compiler_params=pltpu.CompilerParams(vmem_limit_bytes=4 << 20),
        name="start",
    )(pltpu.with_memory_space_constraint(state, pltpu.HBM), pltpu.with_memory_space_constraint(levels, pltpu.HBM))
    xbelow = shifted(xhi, "slab", 1)
    xabove = shifted(xlo, "slab", -1)
    zbelow = shifted(zhi, "curve", 1)
    zabove = shifted(zlo, "curve", -1)
    peak = exchanged(peak, planes)
    a, b, to_left, to_right, peak = pl.pallas_call(
        middle_kernel,
        out_shape=(block, block, block, block, shape(len(columns[0]), 1, EL)),
        in_specs=[VMEM] * 13,
        out_specs=(VMEM,) * 5,
        scratch_shapes=[
            pltpu.VMEM((NV * FPAD, EL), jnp.float32),
            pltpu.VMEM((NV * FPAD, EL), jnp.float32),
            pltpu.VMEM((3 * PAD + 6 * FPAD, NV * EL), jnp.float32),
            pltpu.VMEM((6 * FPAD, NV * EL), jnp.float32),
        ],
        compiler_params=pltpu.CompilerParams(vmem_limit_bytes=12 << 20),
        name="middle",
    )(
        u, xlo, xhi, zlo, zhi, xbelow, xabove, zbelow, zabove, neighbours, scale, peak, operator
    )
    from_left = shifted(to_right, "curve", 1)
    from_right = shifted(to_left, "curve", -1)
    peak = exchanged(peak, columns)
    return pl.pallas_call(
        last_kernel,
        out_shape=(shape(NV, NODES, 1, EL), shape(NV, FACE, 1, EL)),
        in_specs=[SMEM] + [VMEM] * 6,
        out_specs=(ANY, ANY),
        scratch_shapes=[
            pltpu.VMEM((NV, PAD, EL), jnp.float32),
            pltpu.VMEM((NV, FPAD, EL), jnp.float32),
            pltpu.SemaphoreType.DMA((2 * NV,)),
        ],
        compiler_params=pltpu.CompilerParams(vmem_limit_bytes=8 << 20),
        name="last",
    )(shifts, u, a, b, from_left, from_right, peak)


def solution(mesh):
    placed = (
        P(None, None, "slab", "curve"),
        P("slab", "curve"),
        P(None, "slab", "curve"),
        P("slab", "curve"),
    )
    return jax.shard_map(
        on_device,
        mesh=mesh,
        in_specs=placed,
        out_specs=(P(None, None, "slab", "curve"), P(None, None, "slab", "curve")),
        check_vma=False,
    )
```

```python
import jax
import jax.numpy as jnp
import numpy as np
from jax import lax
from jax.experimental import pallas as pl
from jax.experimental.pallas import tpu as pltpu
from jax.sharding import PartitionSpec as P


NV = 5
NODES = 125
FACE = 25
EL = 128
GAMMA = 1.4
CFL = 0.05
END_WEIGHT = 0.1
PAD = 128
FPAD = 32
LANES = 42
Z, Y, X, CORES = 12, 8, 4, 2
HIGH = lax.Precision.HIGHEST
AXES = ("curve", "slab")


def flat(z, y, x, core):
    return (z * Y + y) * X * CORES + x * CORES + core


def plane_groups():
    return [
        [flat(z, y, x, c) for y in range(Y) for x in range(X)] for z in range(Z) for c in range(CORES)
    ]


def column_groups():
    return [
        [flat(z, y, x, c) for z in range(Z) for c in range(CORES)] for y in range(Y) for x in range(X)
    ]


def derivative_matrix():
    points = np.array([-1.0, -np.sqrt(3.0 / 7.0), 0.0, np.sqrt(3.0 / 7.0), 1.0])
    bary = np.array(
        [1.0 / np.prod([points[j] - points[k] for k in range(5) if k != j]) for j in range(5)]
    )
    table = np.zeros((5, 5))
    for i in range(5):
        for j in range(5):
            if i != j:
                table[i, j] = bary[j] / bary[i] / (points[i] - points[j])
        table[i, i] = -np.sum(table[i])
    return table


def face_nodes(f):
    d, end = f // 2, 4 * (f % 2)
    nodes = []
    for b in range(5):
        for a in range(5):
            ijk = {0: (end, a, b), 1: (a, end, b), 2: (a, b, end)}[d]
            nodes.append(ijk[0] + 5 * ijk[1] + 25 * ijk[2])
    return nodes


def operator_table():
    half = 0.5 / END_WEIGHT
    table = derivative_matrix()
    eye = np.eye(5)
    volume = np.zeros((PAD, 3 * PAD))
    for d, parts in enumerate(((eye, eye, table), (eye, table, eye), (table, eye, eye))):
        full = np.kron(parts[0], np.kron(parts[1], parts[2]))
        volume[:NODES, d * PAD : d * PAD + NODES] = -full
    place = np.zeros((PAD, 6 * FPAD))
    count = np.zeros((PAD, 1))
    for f in range(6):
        sign = 1.0 - 2.0 * (f % 2)
        for m, n in enumerate(face_nodes(f)):
            place[n, f * FPAD + m] = 1.0
            volume[n, (f // 2) * PAD + n] -= sign * half
            count[n, 0] += half
    return np.concatenate([volume, place, np.broadcast_to(count, (PAD, EL))], axis=1).astype(np.float32)


def flux(u, d):
    density, momentum, energy = u[0], u[1:4], u[4]
    inverse = 1.0 / density
    velocity = [m * inverse for m in momentum]
    kinetic = momentum[0] * velocity[0] + momentum[1] * velocity[1] + momentum[2] * velocity[2]
    press = (GAMMA - 1.0) * (energy - 0.5 * kinetic)
    along = velocity[d]
    parts = [momentum[d]]
    for a in range(3):
        term = momentum[a] * along
        parts.append(term + press if a == d else term)
    parts.append((energy + press) * along)
    return parts


def all_fluxes(u):
    density, momentum, energy = u[0], u[1:4], u[4]
    inverse = 1.0 / density
    velocity = [m * inverse for m in momentum]
    kinetic = momentum[0] * velocity[0] + momentum[1] * velocity[1] + momentum[2] * velocity[2]
    press = (GAMMA - 1.0) * (energy - 0.5 * kinetic)
    total = energy + press
    out = []
    for d in range(3):
        along = velocity[d]
        parts = [momentum[d]]
        for a in range(3):
            term = momentum[a] * along
            parts.append(term + press if a == d else term)
        parts.append(total * along)
        out.append(parts)
    return out


def lane_pair(lam, top):
    lane = lax.broadcasted_iota(jnp.int32, (1, EL), 1)
    return jnp.where(lane < EL // 2, lam, top)


def start_kernel(state, levels, u, scale_row, peak, xlo, xhi, zlo, zhi, level, sem):
    copies = [
        pltpu.make_async_copy(state.at[v, :, 0], u.at[v, pl.ds(0, NODES)], sem.at[v]) for v in range(NV)
    ]
    copies.append(pltpu.make_async_copy(levels, level, sem.at[NV]))
    for copy in copies:
        copy.start()
    for v in range(NV):
        u[v, NODES:PAD, :] = jnp.full((PAD - NODES, EL), 1.0 if v == 0 else 0.0, jnp.float32)
    for copy in copies:
        copy.wait()
    scale = jnp.exp2(level[...].astype(jnp.float32))
    scale_row[...] = scale
    density, energy = u[0], u[4]
    momentum = [u[1], u[2], u[3]]
    inverse = 1.0 / density
    velocity = [m * inverse for m in momentum]
    kinetic = momentum[0] * velocity[0] + momentum[1] * velocity[1] + momentum[2] * velocity[2]
    press = (GAMMA - 1.0) * (energy - 0.5 * kinetic)
    square = velocity[0] * velocity[0] + velocity[1] * velocity[1] + velocity[2] * velocity[2]
    speed = jnp.sqrt(square) + jnp.sqrt(GAMMA * press * inverse)
    speed = jnp.max(speed, axis=0, keepdims=True)
    lam = jnp.max(speed, axis=1, keepdims=True)
    top = jnp.max(speed * scale, axis=1, keepdims=True)
    peak[...] = jnp.broadcast_to(lane_pair(lam, top)[None], peak.shape)
    ones = jnp.full((FPAD - FACE, EL), 1.0, jnp.float32)
    for v in range(NV):
        row = v * FPAD
        xlo[row : row + FACE, :] = u[v, pl.ds(0, FACE, stride=5), :]
        xhi[row : row + FACE, :] = u[v, pl.ds(4, FACE, stride=5), :]
        zlo[row : row + FACE, :] = u[v, 0:FACE, :]
        zhi[row : row + FACE, :] = u[v, NODES - FACE : NODES, :]
        for ref in (xlo, xhi, zlo, zhi):
            ref[row + FACE : row + FPAD, :] = ones


def dot(a, b):
    return jnp.dot(a, b, precision=HIGH, preferred_element_type=jnp.float32)


def middle_kernel(
    u, xlo, xhi, zlo, zhi, xbelow, xabove, zbelow, zabove, neighbours, scale_row, peaks, operator,
    a_out, b_out, to_left, to_right, peak, ylo, yhi, rhs, outer, named, table, sem,
):
    fetches = [
        pltpu.make_async_copy(neighbours, named, sem.at[0]),
        pltpu.make_async_copy(operator, table, sem.at[1]),
    ]
    for fetch in fetches:
        fetch.start()
    best = jnp.max(peaks[...], axis=0)
    peak[...] = jnp.broadcast_to(best[None], peak.shape)
    scale = scale_row[...]
    ones = jnp.full((FPAD - FACE, EL), 1.0, jnp.float32)
    for v in range(NV):
        row = v * FPAD
        for k in range(5):
            ylo[row + 5 * k : row + 5 * k + 5, :] = u[v, 25 * k : 25 * k + 5, :]
            yhi[row + 5 * k : row + 5 * k + 5, :] = u[v, 25 * k + 20 : 25 * k + 25, :]
        ylo[row + FACE : row + FPAD, :] = ones
        yhi[row + FACE : row + FPAD, :] = ones
    for d, parts in enumerate(all_fluxes([u[v] for v in range(NV)])):
        for v in range(NV):
            rhs[d * PAD : (d + 1) * PAD, v * EL : (v + 1) * EL] = parts[v]
    source = lax.broadcasted_iota(jnp.int32, (EL, EL), 0)
    fetches[0].wait()
    home = named[2] >> 7
    half = 0.5 / END_WEIGHT
    for f in range(6):
        offset = named[f] & (EL - 1)
        if f < 4:
            trace = (xbelow, xabove, yhi, ylo)[f]
            got = dot(trace[...], (source == offset).astype(jnp.float32))
        else:
            here = (named[f] >> 7) == home
            mine, other = ((zhi, zbelow), (zlo, zabove))[f - 4]
            own_index = jnp.where(here, offset, -1)
            other_index = jnp.where(here, -1, offset)
            got = dot(mine[...], (source == own_index).astype(jnp.float32)) + dot(
                other[...], (source == other_index).astype(jnp.float32)
            )
        got = [got[v * FPAD : (v + 1) * FPAD] for v in range(NV)]
        sign = half * (1.0 - 2.0 * (f % 2))
        parts = flux(got, f // 2)
        for v in range(NV):
            rhs[3 * PAD + f * FPAD : 3 * PAD + (f + 1) * FPAD, v * EL : (v + 1) * EL] = sign * parts[v]
            outer[f * FPAD : (f + 1) * FPAD, v * EL : (v + 1) * EL] = half * got[v]
    place = 3 * PAD + 6 * FPAD
    fetches[1].wait()
    a = dot(table[:, :place], rhs[...])
    b = dot(table[:, 3 * PAD : place], outer[...])
    count = table[:, place:]
    lane = lax.broadcasted_iota(jnp.int32, (PAD, EL), 1)
    for v in range(NV):
        uv = u[v]
        av = a[:, v * EL : (v + 1) * EL] * scale
        bv = (b[:, v * EL : (v + 1) * EL] - count * uv) * scale
        a_out[v] = av
        b_out[v] = bv
        to_left[v] = jnp.where(
            lane < LANES,
            uv,
            jnp.where(lane < 2 * LANES, pltpu.roll(av, LANES, 1), pltpu.roll(bv, 2 * LANES, 1)),
        )
        to_right[v] = jnp.where(
            lane < LANES,
            pltpu.roll(uv, LANES, 1),
            jnp.where(lane < 2 * LANES, pltpu.roll(av, 2 * LANES, 1), pltpu.roll(bv, 3 * LANES, 1)),
        )


def last_kernel(shifts, u, a, b, from_left, from_right, peaks, moved, mortar, new, surface, sem):
    best = jnp.max(peaks[...], axis=0)
    lam = jnp.max(best[:, : EL // 2], axis=1, keepdims=True)
    top = jnp.max(best[:, EL // 2 :], axis=1, keepdims=True)
    step = CFL / top
    shift = shifts[0, 0]
    ahead = shift >= 1
    turn = jnp.where(ahead, 2 * EL - shift, 2 * EL - shift - LANES) % EL
    own_turn = (2 * EL - shift) % EL
    lane = lax.broadcasted_iota(jnp.int32, (PAD, EL), 1)
    first = jnp.where(ahead, EL - shift, 0)
    end = jnp.where(ahead, EL, -shift)
    outside = (lane >= first) & (lane < end)
    lane_up = lax.broadcasted_iota(jnp.int32, (FPAD, EL), 1)
    outside_up = (lane_up >= jnp.where(ahead, first + 1, 0)) & (lane_up < end + 1)
    low, high = [], []
    copies = []
    for v in range(NV):
        own = u[v] + step * (a[v] + lam * b[v])
        pack = jnp.where(ahead, from_right[v], from_left[v])
        halo = pack + step * (pltpu.roll(pack, EL - LANES, 1) + lam * pltpu.roll(pack, EL - 2 * LANES, 1))
        own = pltpu.roll(own, own_turn, 1)
        halo = pltpu.roll(halo, turn, 1)
        block = jnp.where(outside, halo, own)
        new[v] = block
        copy = pltpu.make_async_copy(new.at[v, pl.ds(0, NODES)], moved.at[v, :, 0], sem.at[v])
        copy.start()
        copies.append(copy)
        low.append(block[:FPAD])
        before = jnp.where(
            outside_up, pltpu.roll(halo[PAD - FPAD :], 1, 1), pltpu.roll(own[PAD - FPAD :], 1, 1)
        )
        high.append(pltpu.roll(before, FPAD - 4, 0))
    lower, upper = flux(high, 2), flux(low, 2)
    for v in range(NV):
        surface[v] = 0.5 * (lower[v] + upper[v]) - 0.5 * lam * (low[v] - high[v])
        copy = pltpu.make_async_copy(
            surface.at[v, pl.ds(0, FACE)], mortar.at[v, :, 0], sem.at[NV + v]
        )
        copy.start()
        copies.append(copy)
    for copy in copies:
        copy.wait()


def shape(*dims):
    return jax.ShapeDtypeStruct(dims, jnp.float32)


VMEM = pl.BlockSpec(memory_space=pltpu.VMEM)
ANY = pl.BlockSpec(memory_space=pl.ANY)
HBM = pl.BlockSpec(memory_space=pltpu.HBM)
SMEM = pl.BlockSpec(memory_space=pltpu.SMEM)


def held(value):
    return pltpu.with_memory_space_constraint(value, pltpu.HBM)


def shifted(value, axis, step):
    count = lax.axis_size(axis)
    return lax.ppermute(value, axis, [(i, (i + step) % count) for i in range(count)])


def exchanged(value, groups):
    return lax.all_to_all(value, AXES, 0, 0, tiled=True, axis_index_groups=groups)


def substep(state, levels, neighbours, shifts):
    planes, columns = plane_groups(), column_groups()
    operator = jnp.asarray(operator_table())
    trace = shape(NV * FPAD, EL)
    block = shape(NV, PAD, EL)
    u, scale, peak, xlo, xhi, zlo, zhi = pl.pallas_call(
        start_kernel,
        out_shape=(block, shape(1, EL), shape(len(planes[0]), 1, EL), trace, trace, trace, trace),
        in_specs=[HBM, HBM],
        out_specs=(VMEM,) * 7,
        scratch_shapes=[pltpu.VMEM((1, EL), jnp.int32), pltpu.SemaphoreType.DMA((NV + 1,))],
        compiler_params=pltpu.CompilerParams(vmem_limit_bytes=4 << 20),
        name="start",
    )(held(state), held(levels))
    peak = exchanged(peak, planes)
    xbelow = shifted(xhi, "slab", 1)
    xabove = shifted(xlo, "slab", -1)
    zbelow = shifted(zhi, "curve", 1)
    zabove = shifted(zlo, "curve", -1)
    a, b, to_left, to_right, peak = pl.pallas_call(
        middle_kernel,
        out_shape=(block, block, block, block, shape(len(columns[0]), 1, EL)),
        in_specs=[VMEM] * 9 + [HBM] + [VMEM] * 2 + [HBM],
        out_specs=(VMEM,) * 5,
        scratch_shapes=[
            pltpu.VMEM((NV * FPAD, EL), jnp.float32),
            pltpu.VMEM((NV * FPAD, EL), jnp.float32),
            pltpu.VMEM((3 * PAD + 6 * FPAD, NV * EL), jnp.float32),
            pltpu.VMEM((6 * FPAD, NV * EL), jnp.float32),
            pltpu.VMEM((6, 1, EL), jnp.int32),
            pltpu.VMEM(operator.shape, jnp.float32),
            pltpu.SemaphoreType.DMA((2,)),
        ],
        compiler_params=pltpu.CompilerParams(vmem_limit_bytes=12 << 20),
        name="middle",
    )(
        u, xlo, xhi, zlo, zhi, xbelow, xabove, zbelow, zabove, held(neighbours), scale, peak, held(operator)
    )
    peak = exchanged(peak, columns)
    from_left = shifted(to_right, "curve", 1)
    from_right = shifted(to_left, "curve", -1)
    return pl.pallas_call(
        last_kernel,
        out_shape=(shape(NV, NODES, 1, EL), shape(NV, FACE, 1, EL)),
        in_specs=[SMEM] + [VMEM] * 6,
        out_specs=(ANY, ANY),
        scratch_shapes=[
            pltpu.VMEM((NV, PAD, EL), jnp.float32),
            pltpu.VMEM((NV, FPAD, EL), jnp.float32),
            pltpu.SemaphoreType.DMA((2 * NV,)),
        ],
        compiler_params=pltpu.CompilerParams(vmem_limit_bytes=8 << 20),
        name="last",
    )(shifts, u, a, b, from_left, from_right, peak)


def solution(mesh):
    placed = (
        P(None, None, "slab", "curve"),
        P("slab", "curve"),
        P(None, "slab", "curve"),
        P("slab", "curve"),
    )
    return jax.shard_map(
        substep,
        mesh=mesh,
        in_specs=placed,
        out_specs=(P(None, None, "slab", "curve"), P(None, None, "slab", "curve")),
        check_vma=False,
    )
```

```python
import jax
import jax.numpy as jnp
import numpy as np
from jax import lax
from jax.experimental import pallas as pl
from jax.experimental.pallas import tpu as pltpu
from jax.sharding import PartitionSpec as P


NV = 5
NODES = 125
FACE = 25
EL = 128
GAMMA = 1.4
CFL = 0.05
END_WEIGHT = 0.1
PAD = 128
FPAD = 32
LANES = 32
SHIFT_MAX = 32
PACK = NV * PAD // 4
Z, Y, X, CORES = 12, 8, 4, 2
HIGH = lax.Precision.HIGHEST
AXES = ("curve", "slab")


def flat(z, y, x, core):
    return (z * Y + y) * X * CORES + x * CORES + core


def plane_groups():
    return [
        [flat(z, y, x, c) for y in range(Y) for x in range(X)] for z in range(Z) for c in range(CORES)
    ]


def column_groups():
    return [
        [flat(z, y, x, c) for z in range(Z) for c in range(CORES)] for y in range(Y) for x in range(X)
    ]


def derivative_matrix():
    points = np.array([-1.0, -np.sqrt(3.0 / 7.0), 0.0, np.sqrt(3.0 / 7.0), 1.0])
    bary = np.array(
        [1.0 / np.prod([points[j] - points[k] for k in range(5) if k != j]) for j in range(5)]
    )
    table = np.zeros((5, 5))
    for i in range(5):
        for j in range(5):
            if i != j:
                table[i, j] = bary[j] / bary[i] / (points[i] - points[j])
        table[i, i] = -np.sum(table[i])
    return table


def face_nodes(f):
    d, end = f // 2, 4 * (f % 2)
    nodes = []
    for b in range(5):
        for a in range(5):
            ijk = {0: (end, a, b), 1: (a, end, b), 2: (a, b, end)}[d]
            nodes.append(ijk[0] + 5 * ijk[1] + 25 * ijk[2])
    return nodes


def operator_table():
    half = 0.5 / END_WEIGHT
    table = derivative_matrix()
    eye = np.eye(5)
    volume = np.zeros((PAD, 3 * PAD))
    for d, parts in enumerate(((eye, eye, table), (eye, table, eye), (table, eye, eye))):
        full = np.kron(parts[0], np.kron(parts[1], parts[2]))
        volume[:NODES, d * PAD : d * PAD + NODES] = -full
    place = np.zeros((PAD, 6 * FPAD))
    count = np.zeros((PAD, 1))
    for f in range(6):
        sign = 1.0 - 2.0 * (f % 2)
        for m, n in enumerate(face_nodes(f)):
            place[n, f * FPAD + m] = 1.0
            volume[n, (f // 2) * PAD + n] -= sign * half
            count[n, 0] += half
    return np.concatenate([volume, place, np.broadcast_to(count, (PAD, EL))], axis=1).astype(np.float32)


def flux(u, d):
    density, momentum, energy = u[0], u[1:4], u[4]
    inverse = 1.0 / density
    velocity = [m * inverse for m in momentum]
    kinetic = momentum[0] * velocity[0] + momentum[1] * velocity[1] + momentum[2] * velocity[2]
    press = (GAMMA - 1.0) * (energy - 0.5 * kinetic)
    along = velocity[d]
    parts = [momentum[d]]
    for a in range(3):
        term = momentum[a] * along
        parts.append(term + press if a == d else term)
    parts.append((energy + press) * along)
    return parts


def all_fluxes(u):
    density, momentum, energy = u[0], u[1:4], u[4]
    inverse = 1.0 / density
    velocity = [m * inverse for m in momentum]
    kinetic = momentum[0] * velocity[0] + momentum[1] * velocity[1] + momentum[2] * velocity[2]
    press = (GAMMA - 1.0) * (energy - 0.5 * kinetic)
    total = energy + press
    out = []
    for d in range(3):
        along = velocity[d]
        parts = [momentum[d]]
        for a in range(3):
            term = momentum[a] * along
            parts.append(term + press if a == d else term)
        parts.append(total * along)
        out.append(parts)
    return out


def lane_pair(lam, top):
    lane = lax.broadcasted_iota(jnp.int32, (1, EL), 1)
    return jnp.where(lane < EL // 2, lam, top)


def packed(source, out, base, first):
    lane = lax.broadcasted_iota(jnp.int32, (PACK, EL), 1)
    total = None
    for g in range(4):
        rows, row = [], g * PACK
        while row < (g + 1) * PACK:
            v, n = row // PAD, row % PAD
            size = min(PAD - n, (g + 1) * PACK - row)
            rows.append(source[v, n : n + size, :])
            row += size
        part = pltpu.roll(jnp.concatenate(rows, axis=0), (LANES * g - first) % EL, 1)
        total = part if g == 0 else jnp.where(lane >= LANES * g, part, total)
    out[base : base + PACK, :] = total


def spread(source, out, base):
    down = lax.broadcasted_iota(jnp.int32, (FPAD, EL), 0)
    lane = lax.broadcasted_iota(jnp.int32, (FPAD, EL), 1)
    for v in range(NV):
        g, row = divmod(v * PAD + NODES, PACK)
        column = source[v, PAD - FPAD : PAD, EL - LANES - 1 : EL - LANES]
        line = jnp.sum(jnp.where(lane - LANES * g == down, column, 0.0), axis=0, keepdims=True)
        at = slice(base + row, base + row + 1)
        inside = (lane[:1] >= LANES * g) & (lane[:1] < LANES * (g + 1))
        out[at, :] = jnp.where(inside, line, out[at, :])


def start_kernel(state, levels, u, scale_row, peak, xlo, xhi, down, up, level, sem):
    copies = [
        pltpu.make_async_copy(state.at[v, :, 0], u.at[v, pl.ds(0, NODES)], sem.at[v]) for v in range(NV)
    ]
    copies.append(pltpu.make_async_copy(levels, level, sem.at[NV]))
    for copy in copies:
        copy.start()
    for v in range(NV):
        u[v, NODES:PAD, :] = jnp.full((PAD - NODES, EL), 1.0 if v == 0 else 0.0, jnp.float32)
    for copy in copies:
        copy.wait()
    scale = jnp.exp2(level[...].astype(jnp.float32))
    scale_row[...] = scale
    density, energy = u[0], u[4]
    momentum = [u[1], u[2], u[3]]
    inverse = 1.0 / density
    velocity = [m * inverse for m in momentum]
    kinetic = momentum[0] * velocity[0] + momentum[1] * velocity[1] + momentum[2] * velocity[2]
    press = (GAMMA - 1.0) * (energy - 0.5 * kinetic)
    square = velocity[0] * velocity[0] + velocity[1] * velocity[1] + velocity[2] * velocity[2]
    speed = jnp.sqrt(square) + jnp.sqrt(GAMMA * press * inverse)
    speed = jnp.max(speed, axis=0, keepdims=True)
    lam = jnp.max(speed, axis=1, keepdims=True)
    top = jnp.max(speed * scale, axis=1, keepdims=True)
    peak[...] = jnp.broadcast_to(lane_pair(lam, top)[None], peak.shape)
    ones = jnp.full((FPAD - FACE, EL), 1.0, jnp.float32)
    for v in range(NV):
        row = v * FPAD
        xlo[row : row + FACE, :] = u[v, pl.ds(0, FACE, stride=5), :]
        xhi[row : row + FACE, :] = u[v, pl.ds(4, FACE, stride=5), :]
        down[row : row + FACE, :] = u[v, 0:FACE, :]
        up[row : row + FACE, :] = u[v, NODES - FACE : NODES, :]
        for ref in (xlo, xhi, down, up):
            ref[row + FACE : row + FPAD, :] = ones
    packed(u, down, NV * FPAD, 0)
    packed(u, up, NV * FPAD, EL - LANES)
    spread(u, up, NV * FPAD)


def dot(a, b):
    return jnp.dot(a, b, precision=HIGH, preferred_element_type=jnp.float32)


def middle_kernel(
    u, xbelow, xabove, up, down, below, above, neighbours, scale_row, operator,
    a_out, b_out, to_left, to_right, ylo, yhi, rhs, outer, named, table, sem,
):
    fetches = [
        pltpu.make_async_copy(neighbours, named, sem.at[0]),
        pltpu.make_async_copy(operator, table, sem.at[1]),
    ]
    for fetch in fetches:
        fetch.start()
    scale = scale_row[...]
    ones = jnp.full((FPAD - FACE, EL), 1.0, jnp.float32)
    for v in range(NV):
        row = v * FPAD
        for k in range(5):
            ylo[row + 5 * k : row + 5 * k + 5, :] = u[v, 25 * k : 25 * k + 5, :]
            yhi[row + 5 * k : row + 5 * k + 5, :] = u[v, 25 * k + 20 : 25 * k + 25, :]
        ylo[row + FACE : row + FPAD, :] = ones
        yhi[row + FACE : row + FPAD, :] = ones
    for d, parts in enumerate(all_fluxes([u[v] for v in range(NV)])):
        for v in range(NV):
            rhs[d * PAD : (d + 1) * PAD, v * EL : (v + 1) * EL] = parts[v]
    source = lax.broadcasted_iota(jnp.int32, (EL, EL), 0)
    fetches[0].wait()
    home = named[2] >> 7
    half = 0.5 / END_WEIGHT
    for f in range(6):
        offset = named[f] & (EL - 1)
        if f < 4:
            trace = (xbelow, xabove, yhi, ylo)[f]
            got = dot(trace[...], (source == offset).astype(jnp.float32))
        else:
            here = (named[f] >> 7) == home
            mine, other = ((up, below), (down, above))[f - 4]
            own_index = jnp.where(here, offset, -1)
            other_index = jnp.where(here, -1, offset)
            got = dot(mine[: NV * FPAD], (source == own_index).astype(jnp.float32)) + dot(
                other[: NV * FPAD], (source == other_index).astype(jnp.float32)
            )
        got = [got[v * FPAD : (v + 1) * FPAD] for v in range(NV)]
        sign = half * (1.0 - 2.0 * (f % 2))
        parts = flux(got, f // 2)
        for v in range(NV):
            rhs[3 * PAD + f * FPAD : 3 * PAD + (f + 1) * FPAD, v * EL : (v + 1) * EL] = sign * parts[v]
            outer[f * FPAD : (f + 1) * FPAD, v * EL : (v + 1) * EL] = half * got[v]
    place = 3 * PAD + 6 * FPAD
    fetches[1].wait()
    a = dot(table[:, :place], rhs[...])
    b = dot(table[:, 3 * PAD : place], outer[...])
    count = table[:, place:]
    for v in range(NV):
        a_out[v] = a[:, v * EL : (v + 1) * EL] * scale
        b_out[v] = (b[:, v * EL : (v + 1) * EL] - count * u[v]) * scale
    for i, ref in enumerate((a_out, b_out)):
        packed(ref, to_left, i * PACK, 0)
        packed(ref, to_right, i * PACK, EL - LANES)
        spread(ref, to_right, i * PACK)


def merge_kernel(peaks, peak):
    best = jnp.max(peaks[...], axis=0)
    peak[...] = jnp.broadcast_to(best[None], peak.shape)


def last_kernel(
    shifts, u, a, b, below, above, from_left, from_right, peaks, moved, mortar, new, surface, halos, sem
):
    best = jnp.max(peaks[...], axis=0)
    lam = jnp.max(best[:, : EL // 2], axis=1, keepdims=True)
    top = jnp.max(best[:, EL // 2 :], axis=1, keepdims=True)
    step = CFL / top
    shift = shifts[0, 0]
    ahead = shift >= 1
    own_turn = (2 * EL - shift) % EL
    lane = lax.broadcasted_iota(jnp.int32, (PAD, EL), 1)
    first = jnp.where(ahead, EL - shift, 0)
    end = jnp.where(ahead, EL, -shift)
    outside = (lane >= first) & (lane < end)
    down = lax.broadcasted_iota(jnp.int32, (FPAD, EL), 0)
    lane_up = lax.broadcasted_iota(jnp.int32, (FPAD, EL), 1)
    outside_up = (lane_up >= jnp.where(ahead, first + 1, 0)) & (lane_up < end + 1)
    far = lane_up < jnp.where(shift == -SHIFT_MAX, 1, 0)
    trace = slice(NV * FPAD, NV * FPAD + PACK)
    pack = jnp.where(ahead, above[trace, :], below[trace, :])
    rate = jnp.where(ahead, from_right[:PACK], from_left[:PACK]) + lam * jnp.where(
        ahead, from_right[PACK:], from_left[PACK:]
    )
    pack = pack + step * rate
    back = jnp.where(ahead, 0, LANES) + shift
    for g in range(4):
        halos[g * PACK : (g + 1) * PACK, :] = pltpu.roll(pack, (2 * EL - LANES * g - back) % EL, 1)
    low, high = [], []
    copies = []
    for v in range(NV):
        own = pltpu.roll(u[v] + step * (a[v] + lam * b[v]), own_turn, 1)
        halo = halos[v * PAD : (v + 1) * PAD, :]
        block = jnp.where(outside, halo, own)
        new[v] = block
        copy = pltpu.make_async_copy(new.at[v, pl.ds(0, NODES)], moved.at[v, :, 0], sem.at[v])
        copy.start()
        copies.append(copy)
        low.append(block[:FPAD])
        before = jnp.where(
            outside_up, pltpu.roll(halo[PAD - FPAD :], 1, 1), pltpu.roll(own[PAD - FPAD :], 1, 1)
        )
        g, row = divmod(v * PAD + NODES, PACK)
        line = pack[row : row + 1, :]
        column = jnp.sum(jnp.where(lane_up - LANES * g == down, line, 0.0), axis=1, keepdims=True)
        before = jnp.where(far, column, before)
        high.append(pltpu.roll(before, FPAD - 4, 0))
    lower, upper = flux(high, 2), flux(low, 2)
    for v in range(NV):
        surface[v] = 0.5 * (lower[v] + upper[v]) - 0.5 * lam * (low[v] - high[v])
        copy = pltpu.make_async_copy(
            surface.at[v, pl.ds(0, FACE)], mortar.at[v, :, 0], sem.at[NV + v]
        )
        copy.start()
        copies.append(copy)
    for copy in copies:
        copy.wait()


def shape(*dims):
    return jax.ShapeDtypeStruct(dims, jnp.float32)


VMEM = pl.BlockSpec(memory_space=pltpu.VMEM)
ANY = pl.BlockSpec(memory_space=pl.ANY)
HBM = pl.BlockSpec(memory_space=pltpu.HBM)
SMEM = pl.BlockSpec(memory_space=pltpu.SMEM)


def held(value):
    return pltpu.with_memory_space_constraint(value, pltpu.HBM)


def shifted(value, axis, step):
    count = lax.axis_size(axis)
    return lax.ppermute(value, axis, [(i, (i + step) % count) for i in range(count)])


def exchanged(value, groups):
    return lax.all_to_all(value, AXES, 0, 0, tiled=True, axis_index_groups=groups)


def substep(state, levels, neighbours, shifts):
    planes, columns = plane_groups(), column_groups()
    operator = jnp.asarray(operator_table())
    trace = shape(NV * FPAD, EL)
    edge = shape(NV * FPAD + PACK, EL)
    halo = shape(2 * PACK, EL)
    block = shape(NV, PAD, EL)
    u, scale, peak, xlo, xhi, down, up = pl.pallas_call(
        start_kernel,
        out_shape=(block, shape(1, EL), shape(len(planes[0]), 1, EL), trace, trace, edge, edge),
        in_specs=[HBM, HBM],
        out_specs=(VMEM,) * 7,
        scratch_shapes=[pltpu.VMEM((1, EL), jnp.int32), pltpu.SemaphoreType.DMA((NV + 1,))],
        compiler_params=pltpu.CompilerParams(vmem_limit_bytes=4 << 20),
        name="start",
    )(held(state), held(levels))
    peak = exchanged(peak, planes)
    xbelow = shifted(xhi, "slab", 1)
    xabove = shifted(xlo, "slab", -1)
    below = shifted(up, "curve", 1)
    above = shifted(down, "curve", -1)
    a, b, to_left, to_right = pl.pallas_call(
        middle_kernel,
        out_shape=(block, block, halo, halo),
        in_specs=[VMEM] * 7 + [HBM, VMEM, HBM],
        out_specs=(VMEM,) * 4,
        scratch_shapes=[
            pltpu.VMEM((NV * FPAD, EL), jnp.float32),
            pltpu.VMEM((NV * FPAD, EL), jnp.float32),
            pltpu.VMEM((3 * PAD + 6 * FPAD, NV * EL), jnp.float32),
            pltpu.VMEM((6 * FPAD, NV * EL), jnp.float32),
            pltpu.VMEM((6, 1, EL), jnp.int32),
            pltpu.VMEM(operator.shape, jnp.float32),
            pltpu.SemaphoreType.DMA((2,)),
        ],
        compiler_params=pltpu.CompilerParams(vmem_limit_bytes=12 << 20),
        name="middle",
    )(
        u, xbelow, xabove, up, down, below, above, held(neighbours), scale, held(operator)
    )
    peak = pl.pallas_call(
        merge_kernel,
        out_shape=shape(len(columns[0]), 1, EL),
        in_specs=[VMEM],
        out_specs=VMEM,
        compiler_params=pltpu.CompilerParams(vmem_limit_bytes=1 << 20),
        name="merge",
    )(peak)
    peak = exchanged(peak, columns)
    from_left = shifted(to_right, "curve", 1)
    from_right = shifted(to_left, "curve", -1)
    return pl.pallas_call(
        last_kernel,
        out_shape=(shape(NV, NODES, 1, EL), shape(NV, FACE, 1, EL)),
        in_specs=[SMEM] + [VMEM] * 8,
        out_specs=(ANY, ANY),
        scratch_shapes=[
            pltpu.VMEM((NV, PAD, EL), jnp.float32),
            pltpu.VMEM((NV, FPAD, EL), jnp.float32),
            pltpu.VMEM((NV * PAD, EL), jnp.float32),
            pltpu.SemaphoreType.DMA((2 * NV,)),
        ],
        compiler_params=pltpu.CompilerParams(vmem_limit_bytes=8 << 20),
        name="last",
    )(shifts, u, a, b, below, above, from_left, from_right, peak)


def solution(mesh):
    placed = (
        P(None, None, "slab", "curve"),
        P("slab", "curve"),
        P(None, "slab", "curve"),
        P("slab", "curve"),
    )
    return jax.shard_map(
        substep,
        mesh=mesh,
        in_specs=placed,
        out_specs=(P(None, None, "slab", "curve"), P(None, None, "slab", "curve")),
        check_vma=False,
    )
```

```python
import jax
import jax.numpy as jnp
import numpy as np
from jax import lax
from jax.experimental import pallas as pl
from jax.experimental.pallas import tpu as pltpu
from jax.sharding import PartitionSpec as P


NV = 5
NODES = 125
FACE = 25
EL = 128
GAMMA = 1.4
CFL = 0.05
END_WEIGHT = 0.1
PAD = 128
FPAD = 32
LANES = 32
SHIFT_MAX = 32
PACK = NV * PAD // 4
Z, Y, X, CORES = 12, 8, 4, 2
AXES = ("curve", "slab")


def flat(z, y, x, core):
    return (z * Y + y) * X * CORES + x * CORES + core


def plane_groups():
    return [
        [flat(z, y, x, c) for y in range(Y) for x in range(X)] for z in range(Z) for c in range(CORES)
    ]


def column_groups():
    return [
        [flat(z, y, x, c) for z in range(Z) for c in range(CORES)] for y in range(Y) for x in range(X)
    ]


def derivative_matrix():
    points = np.array([-1.0, -np.sqrt(3.0 / 7.0), 0.0, np.sqrt(3.0 / 7.0), 1.0])
    bary = np.array(
        [1.0 / np.prod([points[j] - points[k] for k in range(5) if k != j]) for j in range(5)]
    )
    table = np.zeros((5, 5))
    for i in range(5):
        for j in range(5):
            if i != j:
                table[i, j] = bary[j] / bary[i] / (points[i] - points[j])
        table[i, i] = -np.sum(table[i])
    return table


def face_nodes(f):
    d, end = f // 2, 4 * (f % 2)
    nodes = []
    for b in range(5):
        for a in range(5):
            ijk = {0: (end, a, b), 1: (a, end, b), 2: (a, b, end)}[d]
            nodes.append(ijk[0] + 5 * ijk[1] + 25 * ijk[2])
    return nodes


def operator_table():
    half = 0.5 / END_WEIGHT
    table = derivative_matrix()
    eye = np.eye(5)
    volume = np.zeros((PAD, 3 * PAD))
    for d, parts in enumerate(((eye, eye, table), (eye, table, eye), (table, eye, eye))):
        full = np.kron(parts[0], np.kron(parts[1], parts[2]))
        volume[:NODES, d * PAD : d * PAD + NODES] = -full
    place = np.zeros((PAD, 6 * FPAD))
    for f in range(6):
        sign = 1.0 - 2.0 * (f % 2)
        for m, n in enumerate(face_nodes(f)):
            place[n, f * FPAD + m] = 1.0
            volume[n, (f // 2) * PAD + n] -= sign * half
    top = volume.astype(jnp.bfloat16)
    rest = (volume - top.astype(np.float64)).astype(jnp.bfloat16)
    place = place.astype(jnp.bfloat16)
    return np.concatenate([np.concatenate([top, place], axis=1), np.concatenate([rest, place], axis=1)])


def flux(u, d):
    density, momentum, energy = u[0], u[1:4], u[4]
    inverse = 1.0 / density
    velocity = [m * inverse for m in momentum]
    kinetic = momentum[0] * velocity[0] + momentum[1] * velocity[1] + momentum[2] * velocity[2]
    press = (GAMMA - 1.0) * (energy - 0.5 * kinetic)
    along = velocity[d]
    parts = [momentum[d]]
    for a in range(3):
        term = momentum[a] * along
        parts.append(term + press if a == d else term)
    parts.append((energy + press) * along)
    return parts


def all_fluxes(u):
    density, momentum, energy = u[0], u[1:4], u[4]
    inverse = 1.0 / density
    velocity = [m * inverse for m in momentum]
    kinetic = momentum[0] * velocity[0] + momentum[1] * velocity[1] + momentum[2] * velocity[2]
    press = (GAMMA - 1.0) * (energy - 0.5 * kinetic)
    total = energy + press
    out = []
    for d in range(3):
        along = velocity[d]
        parts = [momentum[d]]
        for a in range(3):
            term = momentum[a] * along
            parts.append(term + press if a == d else term)
        parts.append(total * along)
        out.append(parts)
    return out


def lane_pair(lam, top):
    lane = lax.broadcasted_iota(jnp.int32, (1, EL), 1)
    return jnp.where(lane < EL // 2, lam, top)


def packed(source, out, base, first):
    lane = lax.broadcasted_iota(jnp.int32, (PACK, EL), 1)
    total = None
    for g in range(4):
        rows, row = [], g * PACK
        while row < (g + 1) * PACK:
            v, n = row // PAD, row % PAD
            size = min(PAD - n, (g + 1) * PACK - row)
            rows.append(source[v, n : n + size, :])
            row += size
        part = pltpu.roll(jnp.concatenate(rows, axis=0), (LANES * g - first) % EL, 1)
        total = part if g == 0 else jnp.where(lane >= LANES * g, part, total)
    out[base : base + PACK, :] = total


def spread(source, out, base):
    down = lax.broadcasted_iota(jnp.int32, (FPAD, EL), 0)
    lane = lax.broadcasted_iota(jnp.int32, (FPAD, EL), 1)
    for v in range(NV):
        g, row = divmod(v * PAD + NODES, PACK)
        column = source[v, PAD - FPAD : PAD, EL - LANES - 1 : EL - LANES]
        line = jnp.sum(jnp.where(lane - LANES * g == down, column, 0.0), axis=0, keepdims=True)
        at = slice(base + row, base + row + 1)
        inside = (lane[:1] >= LANES * g) & (lane[:1] < LANES * (g + 1))
        out[at, :] = jnp.where(inside, line, out[at, :])


def start_kernel(state, levels, u, scale_row, peak, xlo, xhi, down, up, level, best, sem):
    copies = [
        pltpu.make_async_copy(state.at[v, :, 0], u.at[v, pl.ds(0, NODES)], sem.at[v]) for v in range(NV)
    ]
    copies.append(pltpu.make_async_copy(levels, level, sem.at[NV]))
    for copy in copies:
        copy.start()
    for v in range(NV):
        u[v, NODES:PAD, :] = jnp.full((PAD - NODES, EL), 1.0 if v == 0 else 0.0, jnp.float32)
    for copy in copies:
        copy.wait()
    scale = jnp.exp2(level[...].astype(jnp.float32))
    scale_row[...] = scale
    density, energy = u[0], u[4]
    momentum = [u[1], u[2], u[3]]
    inverse = 1.0 / density
    velocity = [m * inverse for m in momentum]
    kinetic = momentum[0] * velocity[0] + momentum[1] * velocity[1] + momentum[2] * velocity[2]
    press = (GAMMA - 1.0) * (energy - 0.5 * kinetic)
    square = velocity[0] * velocity[0] + velocity[1] * velocity[1] + velocity[2] * velocity[2]
    speed = jnp.sqrt(square) + jnp.sqrt(GAMMA * press * inverse)
    speed = jnp.max(speed, axis=0, keepdims=True)
    lam = jnp.max(speed, axis=1, keepdims=True)
    top = jnp.max(speed * scale, axis=1, keepdims=True)
    best[...] = jnp.broadcast_to(lane_pair(lam, top)[None], best.shape)
    send = pltpu.make_async_copy(best, peak, sem.at[NV + 1])
    send.start()
    ones = jnp.full((FPAD - FACE, EL), 1.0, jnp.float32)
    for v in range(NV):
        row = v * FPAD
        xlo[row : row + FACE, :] = u[v, pl.ds(0, FACE, stride=5), :]
        xhi[row : row + FACE, :] = u[v, pl.ds(4, FACE, stride=5), :]
        down[row : row + FACE, :] = u[v, 0:FACE, :]
        up[row : row + FACE, :] = u[v, NODES - FACE : NODES, :]
        for ref in (xlo, xhi, down, up):
            ref[row + FACE : row + FPAD, :] = ones
    packed(u, down, NV * FPAD, 0)
    packed(u, up, NV * FPAD, EL - LANES)
    spread(u, up, NV * FPAD)
    send.wait()


def dot(a, b):
    return jnp.dot(a, b, preferred_element_type=jnp.float32)


def halves(value):
    top = value.astype(jnp.bfloat16)
    return top, (value - top.astype(jnp.float32)).astype(jnp.bfloat16)


def chosen(trace, pick):
    return jnp.take_along_axis(trace, jnp.broadcast_to(pick, trace.shape), axis=1, mode="promise_in_bounds")


def middle_kernel(
    u, xlo, xhi, xbelow, xabove, up, down, below, above, neighbours, scale_row, operator,
    a_out, b_out, to_left, to_right, ylo, yhi, rhs_top, rhs_rest, out_top, out_rest, named, table, sem,
):
    fetches = [
        pltpu.make_async_copy(neighbours, named, sem.at[0]),
        pltpu.make_async_copy(operator, table, sem.at[1]),
    ]
    for fetch in fetches:
        fetch.start()
    scale = scale_row[...]
    ones = jnp.full((FPAD - FACE, EL), 1.0, jnp.float32)
    for v in range(NV):
        row = v * FPAD
        for k in range(5):
            ylo[row + 5 * k : row + 5 * k + 5, :] = u[v, 25 * k : 25 * k + 5, :]
            yhi[row + 5 * k : row + 5 * k + 5, :] = u[v, 25 * k + 20 : 25 * k + 25, :]
        ylo[row + FACE : row + FPAD, :] = ones
        yhi[row + FACE : row + FPAD, :] = ones

    for d, parts in enumerate(all_fluxes([u[v] for v in range(NV)])):
        for v in range(NV):
            at = (slice(d * PAD, (d + 1) * PAD), slice(v * EL, (v + 1) * EL))
            rhs_top[at], rhs_rest[at] = halves(parts[v])
    fetches[0].wait()
    home = named[2] >> 7
    half = 0.5 / END_WEIGHT
    nodes = NV * FPAD
    for f in range(6):
        offset = named[f] & (EL - 1)
        own = (xlo, xhi, ylo, yhi, down, up)[f]
        if f < 4:
            got = chosen((xbelow, xabove, yhi, ylo)[f][...], offset)
        else:
            pick = offset
            mine, other = ((up, below), (down, above))[f - 4]
            here = (named[f] >> 7) == home
            got = jnp.where(here, chosen(mine[:nodes], pick), chosen(other[:nodes], pick))
        sign = half * (1.0 - 2.0 * (f % 2))
        values = [got[v * FPAD : (v + 1) * FPAD] for v in range(NV)]
        parts = flux(values, f // 2)
        rows = slice(f * FPAD, (f + 1) * FPAD)
        for v in range(NV):
            lanes = slice(v * EL, (v + 1) * EL)
            at = (slice(3 * PAD + f * FPAD, 3 * PAD + (f + 1) * FPAD), lanes)
            rhs_top[at], rhs_rest[at] = halves(sign * parts[v])
            jump = half * (values[v] - own[v * FPAD : (v + 1) * FPAD, :])
            out_top[rows, lanes], out_rest[rows, lanes] = halves(jump)
    fetches[1].wait()
    first = dot(table[...][:, : 3 * PAD], rhs_top[: 3 * PAD, :])
    a = first[:PAD] + first[PAD:] + dot(table[:PAD, :], rhs_rest[...])
    a = a + dot(table[:PAD, 3 * PAD :], rhs_top[3 * PAD :, :])
    b = dot(table[:PAD, 3 * PAD :], out_top[...]) + dot(table[:PAD, 3 * PAD :], out_rest[...])
    for v in range(NV):
        a_out[v] = a[:, v * EL : (v + 1) * EL] * scale
        b_out[v] = b[:, v * EL : (v + 1) * EL] * scale
    for i, ref in enumerate((a_out, b_out)):
        packed(ref, to_left, i * PACK, 0)
        packed(ref, to_right, i * PACK, EL - LANES)
        spread(ref, to_right, i * PACK)


def merge_kernel(peaks, peak):
    best = jnp.max(peaks[...], axis=0)
    peak[...] = jnp.broadcast_to(best[None], peak.shape)


def last_kernel(
    shifts, u, a, b, below, above, from_left, from_right, peaks, moved, mortar, new, surface, halos, sem
):
    best = jnp.max(peaks[...], axis=0)
    lam = jnp.max(best[:, : EL // 2], axis=1, keepdims=True)
    top = jnp.max(best[:, EL // 2 :], axis=1, keepdims=True)
    step = CFL / top
    shift = shifts[0, 0]
    ahead = shift >= 1
    own_turn = (2 * EL - shift) % EL
    lane = lax.broadcasted_iota(jnp.int32, (PAD, EL), 1)
    first = jnp.where(ahead, EL - shift, 0)
    end = jnp.where(ahead, EL, -shift)
    outside = (lane >= first) & (lane < end)
    down = lax.broadcasted_iota(jnp.int32, (FPAD, EL), 0)
    lane_up = lax.broadcasted_iota(jnp.int32, (FPAD, EL), 1)
    outside_up = (lane_up >= jnp.where(ahead, first + 1, 0)) & (lane_up < end + 1)
    far = lane_up < jnp.where(shift == -SHIFT_MAX, 1, 0)
    trace = slice(NV * FPAD, NV * FPAD + PACK)
    pack = jnp.where(ahead, above[trace, :], below[trace, :])
    rate = jnp.where(ahead, from_right[:PACK], from_left[:PACK]) + lam * jnp.where(
        ahead, from_right[PACK:], from_left[PACK:]
    )
    pack = pack + step * rate
    back = jnp.where(ahead, 0, LANES) + shift
    for g in range(4):
        halos[g * PACK : (g + 1) * PACK, :] = pltpu.roll(pack, (2 * EL - LANES * g - back) % EL, 1)
    low, high = [], []
    copies = []
    for v in range(NV):
        own = pltpu.roll(u[v] + step * (a[v] + lam * b[v]), own_turn, 1)
        halo = halos[v * PAD : (v + 1) * PAD, :]
        block = jnp.where(outside, halo, own)
        new[v] = block
        copy = pltpu.make_async_copy(new.at[v, pl.ds(0, NODES)], moved.at[v, :, 0], sem.at[v])
        copy.start()
        copies.append(copy)
        low.append(block[:FPAD])
        before = jnp.where(
            outside_up, pltpu.roll(halo[PAD - FPAD :], 1, 1), pltpu.roll(own[PAD - FPAD :], 1, 1)
        )
        g, row = divmod(v * PAD + NODES, PACK)
        line = pack[row : row + 1, :]
        column = jnp.sum(jnp.where(lane_up - LANES * g == down, line, 0.0), axis=1, keepdims=True)
        before = jnp.where(far, column, before)
        high.append(pltpu.roll(before, FPAD - 4, 0))
    lower, upper = flux(high, 2), flux(low, 2)
    for v in range(NV):
        surface[v] = 0.5 * (lower[v] + upper[v]) - 0.5 * lam * (low[v] - high[v])
        copy = pltpu.make_async_copy(
            surface.at[v, pl.ds(0, FACE)], mortar.at[v, :, 0], sem.at[NV + v]
        )
        copy.start()
        copies.append(copy)
    for copy in copies:
        copy.wait()


def shape(*dims):
    return jax.ShapeDtypeStruct(dims, jnp.float32)


VMEM = pl.BlockSpec(memory_space=pltpu.VMEM)
ANY = pl.BlockSpec(memory_space=pl.ANY)
HBM = pl.BlockSpec(memory_space=pltpu.HBM)
SMEM = pl.BlockSpec(memory_space=pltpu.SMEM)


def held(value):
    return pltpu.with_memory_space_constraint(value, pltpu.HBM)


def shifted(value, axis, step):
    count = lax.axis_size(axis)
    return lax.ppermute(value, axis, [(i, (i + step) % count) for i in range(count)])


def exchanged(value, groups):
    return lax.all_to_all(value, AXES, 0, 0, tiled=True, axis_index_groups=groups)


def substep(state, levels, neighbours, shifts):
    planes, columns = column_groups(), plane_groups()
    operator = jnp.asarray(operator_table())
    trace = shape(NV * FPAD, EL)
    edge = shape(NV * FPAD + PACK, EL)
    halo = shape(2 * PACK, EL)
    block = shape(NV, PAD, EL)
    u, scale, peak, xlo, xhi, down, up = pl.pallas_call(
        start_kernel,
        out_shape=(block, shape(1, EL), shape(len(planes[0]), 1, EL), trace, trace, edge, edge),
        in_specs=[HBM, HBM],
        out_specs=(VMEM, VMEM, HBM) + (VMEM,) * 4,
        scratch_shapes=[
            pltpu.VMEM((1, EL), jnp.int32),
            pltpu.VMEM((len(planes[0]), 1, EL), jnp.float32),
            pltpu.SemaphoreType.DMA((NV + 2,)),
        ],
        compiler_params=pltpu.CompilerParams(vmem_limit_bytes=4 << 20),
        name="start",
    )(held(state), held(levels))
    peak = exchanged(peak, planes)
    xbelow = shifted(xhi, "slab", 1)
    xabove = shifted(xlo, "slab", -1)
    below = shifted(up, "curve", 1)
    above = shifted(down, "curve", -1)
    a, b, to_left, to_right = pl.pallas_call(
        middle_kernel,
        out_shape=(block, block, halo, halo),
        in_specs=[VMEM] * 9 + [HBM, VMEM, HBM],
        out_specs=(VMEM,) * 4,
        scratch_shapes=[
            pltpu.VMEM((NV * FPAD, EL), jnp.float32),
            pltpu.VMEM((NV * FPAD, EL), jnp.float32),
            pltpu.VMEM((3 * PAD + 6 * FPAD, NV * EL), jnp.bfloat16),
            pltpu.VMEM((3 * PAD + 6 * FPAD, NV * EL), jnp.bfloat16),
            pltpu.VMEM((6 * FPAD, NV * EL), jnp.bfloat16),
            pltpu.VMEM((6 * FPAD, NV * EL), jnp.bfloat16),
            pltpu.VMEM((6, 1, EL), jnp.int32),
            pltpu.VMEM(operator.shape, jnp.bfloat16),
            pltpu.SemaphoreType.DMA((2,)),
        ],
        compiler_params=pltpu.CompilerParams(vmem_limit_bytes=12 << 20),
        name="middle",
    )(
        u, xlo, xhi, xbelow, xabove, up, down, below, above, held(neighbours), scale, held(operator)
    )
    peak = pl.pallas_call(
        merge_kernel,
        out_shape=shape(len(columns[0]), 1, EL),
        in_specs=[VMEM],
        out_specs=VMEM,
        compiler_params=pltpu.CompilerParams(vmem_limit_bytes=1 << 20),
        name="merge",
    )(peak)
    peak = exchanged(peak, columns)
    from_left = shifted(to_right, "curve", 1)
    from_right = shifted(to_left, "curve", -1)
    return pl.pallas_call(
        last_kernel,
        out_shape=(shape(NV, NODES, 1, EL), shape(NV, FACE, 1, EL)),
        in_specs=[SMEM] + [VMEM] * 8,
        out_specs=(ANY, ANY),
        scratch_shapes=[
            pltpu.VMEM((NV, PAD, EL), jnp.float32),
            pltpu.VMEM((NV, FPAD, EL), jnp.float32),
            pltpu.VMEM((NV * PAD, EL), jnp.float32),
            pltpu.SemaphoreType.DMA((2 * NV,)),
        ],
        compiler_params=pltpu.CompilerParams(vmem_limit_bytes=8 << 20),
        name="last",
    )(shifts, u, a, b, below, above, from_left, from_right, peak)


def solution(mesh):
    placed = (
        P(None, None, "slab", "curve"),
        P("slab", "curve"),
        P(None, "slab", "curve"),
        P("slab", "curve"),
    )
    return jax.shard_map(
        substep,
        mesh=mesh,
        in_specs=placed,
        out_specs=(P(None, None, "slab", "curve"), P(None, None, "slab", "curve")),
        check_vma=False,
    )
```

```python
import jax
import jax.numpy as jnp
import numpy as np
from jax import lax
from jax.experimental import pallas as pl
from jax.experimental.pallas import tpu as pltpu
from jax.sharding import PartitionSpec as P


NV = 5
NODES = 125
FACE = 25
EL = 128
GAMMA = 1.4
CFL = 0.05
END_WEIGHT = 0.1
PAD = 128
FPAD = 32
LANES = 32
SHIFT_MAX = 32
PACK = NV * PAD // 4
Z, Y, X, CORES = 12, 8, 4, 2
AXES = ("curve", "slab")


def flat(z, y, x, core):
    return (z * Y + y) * X * CORES + x * CORES + core


def plane_groups():
    return [
        [flat(z, (y + 6) % Y, (x + 0) % X, c) for y in range(Y) for x in range(X)] for z in range(Z) for c in range(CORES)
    ]


def column_groups():
    return [
        [flat((z + 11) % Z, y, x, c) for z in range(Z) for c in range(CORES)] for y in range(Y) for x in range(X)
    ]


def derivative_matrix():
    points = np.array([-1.0, -np.sqrt(3.0 / 7.0), 0.0, np.sqrt(3.0 / 7.0), 1.0])
    bary = np.array(
        [1.0 / np.prod([points[j] - points[k] for k in range(5) if k != j]) for j in range(5)]
    )
    table = np.zeros((5, 5))
    for i in range(5):
        for j in range(5):
            if i != j:
                table[i, j] = bary[j] / bary[i] / (points[i] - points[j])
        table[i, i] = -np.sum(table[i])
    return table


def face_nodes(f):
    d, end = f // 2, 4 * (f % 2)
    nodes = []
    for b in range(5):
        for a in range(5):
            ijk = {0: (end, a, b), 1: (a, end, b), 2: (a, b, end)}[d]
            nodes.append(ijk[0] + 5 * ijk[1] + 25 * ijk[2])
    return nodes


def operator_table():
    half = 0.5 / END_WEIGHT
    table = derivative_matrix()
    eye = np.eye(5)
    volume = np.zeros((PAD, 3 * PAD))
    for d, parts in enumerate(((eye, eye, table), (eye, table, eye), (table, eye, eye))):
        full = np.kron(parts[0], np.kron(parts[1], parts[2]))
        volume[:NODES, d * PAD : d * PAD + NODES] = -full
    place = np.zeros((PAD, 6 * FPAD))
    for f in range(6):
        sign = 1.0 - 2.0 * (f % 2)
        for m, n in enumerate(face_nodes(f)):
            place[n, f * FPAD + m] = 1.0
            volume[n, (f // 2) * PAD + n] -= sign * half
    top = volume.astype(jnp.bfloat16)
    rest = (volume - top.astype(np.float64)).astype(jnp.bfloat16)
    place = place.astype(jnp.bfloat16)
    return np.concatenate([np.concatenate([top, place], axis=1), np.concatenate([rest, place], axis=1)])


def flux(u, d):
    density, momentum, energy = u[0], u[1:4], u[4]
    inverse = 1.0 / density
    velocity = [m * inverse for m in momentum]
    kinetic = momentum[0] * velocity[0] + momentum[1] * velocity[1] + momentum[2] * velocity[2]
    press = (GAMMA - 1.0) * (energy - 0.5 * kinetic)
    along = velocity[d]
    parts = [momentum[d]]
    for a in range(3):
        term = momentum[a] * along
        parts.append(term + press if a == d else term)
    parts.append((energy + press) * along)
    return parts


def all_fluxes(u):
    density, momentum, energy = u[0], u[1:4], u[4]
    inverse = 1.0 / density
    velocity = [m * inverse for m in momentum]
    kinetic = momentum[0] * velocity[0] + momentum[1] * velocity[1] + momentum[2] * velocity[2]
    press = (GAMMA - 1.0) * (energy - 0.5 * kinetic)
    total = energy + press
    out = []
    for d in range(3):
        along = velocity[d]
        parts = [momentum[d]]
        for a in range(3):
            term = momentum[a] * along
            parts.append(term + press if a == d else term)
        parts.append(total * along)
        out.append(parts)
    return out


def lane_pair(lam, top):
    lane = lax.broadcasted_iota(jnp.int32, (1, EL), 1)
    return jnp.where(lane < EL // 2, lam, top)


def packed(source, out, base, first):
    lane = lax.broadcasted_iota(jnp.int32, (PACK, EL), 1)
    total = None
    for g in range(4):
        rows, row = [], g * PACK
        while row < (g + 1) * PACK:
            v, n = row // PAD, row % PAD
            size = min(PAD - n, (g + 1) * PACK - row)
            rows.append(source[v, n : n + size, :])
            row += size
        part = pltpu.roll(jnp.concatenate(rows, axis=0), (LANES * g - first) % EL, 1)
        total = part if g == 0 else jnp.where(lane >= LANES * g, part, total)
    out[base : base + PACK, :] = total


def spread(source, out, base):
    down = lax.broadcasted_iota(jnp.int32, (FPAD, EL), 0)
    lane = lax.broadcasted_iota(jnp.int32, (FPAD, EL), 1)
    for v in range(NV):
        g, row = divmod(v * PAD + NODES, PACK)
        column = source[v, PAD - FPAD : PAD, EL - LANES - 1 : EL - LANES]
        line = jnp.sum(jnp.where(lane - LANES * g == down, column, 0.0), axis=0, keepdims=True)
        at = slice(base + row, base + row + 1)
        inside = (lane[:1] >= LANES * g) & (lane[:1] < LANES * (g + 1))
        out[at, :] = jnp.where(inside, line, out[at, :])


def first_up():
    return lax.axis_index("curve") % 2 == 1


def start_kernel(state, levels, u, scale_row, peak, xlo, xhi, down, up, level, best, sem):
    copies = [
        pltpu.make_async_copy(state.at[v, :, 0], u.at[v, pl.ds(0, NODES)], sem.at[v]) for v in range(NV)
    ]
    copies.append(pltpu.make_async_copy(levels, level, sem.at[NV]))
    for copy in copies:
        copy.start()
    for v in range(NV):
        u[v, NODES:PAD, :] = jnp.full((PAD - NODES, EL), 1.0 if v == 0 else 0.0, jnp.float32)
    for copy in copies:
        copy.wait()
    scale = jnp.exp2(level[...].astype(jnp.float32))
    scale_row[...] = scale
    density, energy = u[0], u[4]
    momentum = [u[1], u[2], u[3]]
    inverse = 1.0 / density
    velocity = [m * inverse for m in momentum]
    kinetic = momentum[0] * velocity[0] + momentum[1] * velocity[1] + momentum[2] * velocity[2]
    press = (GAMMA - 1.0) * (energy - 0.5 * kinetic)
    square = velocity[0] * velocity[0] + velocity[1] * velocity[1] + velocity[2] * velocity[2]
    speed = jnp.sqrt(square) + jnp.sqrt(GAMMA * press * inverse)
    speed = jnp.max(speed, axis=0, keepdims=True)
    lam = jnp.max(speed, axis=1, keepdims=True)
    top = jnp.max(speed * scale, axis=1, keepdims=True)
    best[...] = jnp.broadcast_to(lane_pair(lam, top)[None], best.shape)
    send = pltpu.make_async_copy(best, peak, sem.at[NV + 1])
    send.start()
    ones = jnp.full((FPAD - FACE, EL), 1.0, jnp.float32)
    for v in range(NV):
        row = v * FPAD
        xlo[row : row + FACE, :] = u[v, pl.ds(0, FACE, stride=5), :]
        xhi[row : row + FACE, :] = u[v, pl.ds(4, FACE, stride=5), :]
        down[row : row + FACE, :] = u[v, 0:FACE, :]
        up[row : row + FACE, :] = u[v, NODES - FACE : NODES, :]
        for ref in (xlo, xhi, down, up):
            ref[row + FACE : row + FPAD, :] = ones
    packed(u, down, NV * FPAD, 0)
    packed(u, up, NV * FPAD, EL - LANES)
    spread(u, up, NV * FPAD)
    send.wait()


def dot(a, b):
    return jnp.dot(a, b, preferred_element_type=jnp.float32)


def halves(value):
    top = value.astype(jnp.bfloat16)
    return top, (value - top.astype(jnp.float32)).astype(jnp.bfloat16)


def chosen(trace, pick):
    return jnp.take_along_axis(trace, jnp.broadcast_to(pick, trace.shape), axis=1, mode="promise_in_bounds")


def middle_kernel(
    u, xlo, xhi, xbelow, xabove, up, down, below, above, neighbours, scale_row, operator,
    a_out, b_out, to_near, to_far, to_left, to_right, ylo, yhi, rhs_top, rhs_rest, out_top, out_rest, named, table, sem,
):
    fetches = [
        pltpu.make_async_copy(neighbours, named, sem.at[0]),
        pltpu.make_async_copy(operator, table, sem.at[1]),
    ]
    for fetch in fetches:
        fetch.start()
    scale = scale_row[...]
    ones = jnp.full((FPAD - FACE, EL), 1.0, jnp.float32)
    for v in range(NV):
        row = v * FPAD
        for k in range(5):
            ylo[row + 5 * k : row + 5 * k + 5, :] = u[v, 25 * k : 25 * k + 5, :]
            yhi[row + 5 * k : row + 5 * k + 5, :] = u[v, 25 * k + 20 : 25 * k + 25, :]
        ylo[row + FACE : row + FPAD, :] = ones
        yhi[row + FACE : row + FPAD, :] = ones

    for d, parts in enumerate(all_fluxes([u[v] for v in range(NV)])):
        for v in range(NV):
            at = (slice(d * PAD, (d + 1) * PAD), slice(v * EL, (v + 1) * EL))
            rhs_top[at], rhs_rest[at] = halves(parts[v])
    fetches[0].wait()
    home = named[2] >> 7
    half = 0.5 / END_WEIGHT
    nodes = NV * FPAD
    for f in range(6):
        offset = named[f] & (EL - 1)
        own = (xlo, xhi, ylo, yhi, down, up)[f]
        if f < 4:
            got = chosen((xbelow, xabove, yhi, ylo)[f][...], offset)
        else:
            pick = offset
            mine, other = ((up, below), (down, above))[f - 4]
            here = (named[f] >> 7) == home
            got = jnp.where(here, chosen(mine[:nodes], pick), chosen(other[:nodes], pick))
        sign = half * (1.0 - 2.0 * (f % 2))
        values = [got[v * FPAD : (v + 1) * FPAD] for v in range(NV)]
        parts = flux(values, f // 2)
        rows = slice(f * FPAD, (f + 1) * FPAD)
        for v in range(NV):
            lanes = slice(v * EL, (v + 1) * EL)
            at = (slice(3 * PAD + f * FPAD, 3 * PAD + (f + 1) * FPAD), lanes)
            rhs_top[at], rhs_rest[at] = halves(sign * parts[v])
            jump = half * (values[v] - own[v * FPAD : (v + 1) * FPAD, :])
            out_top[rows, lanes], out_rest[rows, lanes] = halves(jump)
    fetches[1].wait()
    first = dot(table[...][:, : 3 * PAD], rhs_top[: 3 * PAD, :])
    a = first[:PAD] + first[PAD:] + dot(table[:PAD, :], rhs_rest[...])
    a = a + dot(table[:PAD, 3 * PAD :], rhs_top[3 * PAD :, :])
    b = dot(table[:PAD, 3 * PAD :], out_top[...]) + dot(table[:PAD, 3 * PAD :], out_rest[...])
    for v in range(NV):
        a_out[v] = a[:, v * EL : (v + 1) * EL] * scale
        b_out[v] = b[:, v * EL : (v + 1) * EL] * scale
    for i, ref in enumerate((a_out, b_out)):
        packed(ref, to_left, i * PACK, 0)
        packed(ref, to_right, i * PACK, EL - LANES)
        spread(ref, to_right, i * PACK)
    to_near[...] = jnp.where(first_up(), to_right[...], to_left[...])
    to_far[...] = jnp.where(first_up(), to_left[...], to_right[...])


def merge_kernel(peaks, peak):
    best = jnp.max(peaks[...], axis=0)
    peak[...] = jnp.broadcast_to(best[None], peak.shape)


def last_kernel(
    shifts, u, a, b, below, above, from_near, from_far, peaks, moved, mortar, new, surface, halos, sem
):
    best = jnp.max(peaks[...], axis=0)
    lam = jnp.max(best[:, : EL // 2], axis=1, keepdims=True)
    top = jnp.max(best[:, EL // 2 :], axis=1, keepdims=True)
    step = CFL / top
    shift = shifts[0, 0]
    ahead = shift >= 1
    own_turn = (2 * EL - shift) % EL
    lane = lax.broadcasted_iota(jnp.int32, (PAD, EL), 1)
    first = jnp.where(ahead, EL - shift, 0)
    end = jnp.where(ahead, EL, -shift)
    outside = (lane >= first) & (lane < end)
    down = lax.broadcasted_iota(jnp.int32, (FPAD, EL), 0)
    lane_up = lax.broadcasted_iota(jnp.int32, (FPAD, EL), 1)
    outside_up = (lane_up >= jnp.where(ahead, first + 1, 0)) & (lane_up < end + 1)
    far = lane_up < jnp.where(shift == -SHIFT_MAX, 1, 0)
    trace = slice(NV * FPAD, NV * FPAD + PACK)
    pack = jnp.where(ahead, above[trace, :], below[trace, :])
    nearer = jnp.logical_not(jnp.logical_xor(ahead, first_up()))
    rate = jnp.where(nearer, from_near[:PACK], from_far[:PACK]) + lam * jnp.where(
        nearer, from_near[PACK:], from_far[PACK:]
    )
    pack = pack + step * rate
    back = jnp.where(ahead, 0, LANES) + shift
    for g in range(4):
        halos[g * PACK : (g + 1) * PACK, :] = pltpu.roll(pack, (2 * EL - LANES * g - back) % EL, 1)
    low, high = [], []
    copies = []
    for v in range(NV):
        own = pltpu.roll(u[v] + step * (a[v] + lam * b[v]), own_turn, 1)
        halo = halos[v * PAD : (v + 1) * PAD, :]
        block = jnp.where(outside, halo, own)
        new[v] = block
        copy = pltpu.make_async_copy(new.at[v, pl.ds(0, NODES)], moved.at[v, :, 0], sem.at[v])
        copy.start()
        copies.append(copy)
        low.append(block[:FPAD])
        before = jnp.where(
            outside_up, pltpu.roll(halo[PAD - FPAD :], 1, 1), pltpu.roll(own[PAD - FPAD :], 1, 1)
        )
        g, row = divmod(v * PAD + NODES, PACK)
        line = pack[row : row + 1, :]
        column = jnp.sum(jnp.where(lane_up - LANES * g == down, line, 0.0), axis=1, keepdims=True)
        before = jnp.where(far, column, before)
        high.append(pltpu.roll(before, FPAD - 4, 0))
    lower, upper = flux(high, 2), flux(low, 2)
    for v in range(NV):
        surface[v] = 0.5 * (lower[v] + upper[v]) - 0.5 * lam * (low[v] - high[v])
        copy = pltpu.make_async_copy(
            surface.at[v, pl.ds(0, FACE)], mortar.at[v, :, 0], sem.at[NV + v]
        )
        copy.start()
        copies.append(copy)
    for copy in copies:
        copy.wait()


def shape(*dims):
    return jax.ShapeDtypeStruct(dims, jnp.float32)


VMEM = pl.BlockSpec(memory_space=pltpu.VMEM)
ANY = pl.BlockSpec(memory_space=pl.ANY)
HBM = pl.BlockSpec(memory_space=pltpu.HBM)
SMEM = pl.BlockSpec(memory_space=pltpu.SMEM)


def held(value):
    return pltpu.with_memory_space_constraint(value, pltpu.HBM)


def shifted(value, axis, step):
    count = lax.axis_size(axis)
    return lax.ppermute(value, axis, [(i, (i + step) % count) for i in range(count)])


def swapped(value, start):
    count = lax.axis_size("curve")
    pairs = [(start + k, (start + k + 1) % count) for k in range(0, count, 2)]
    return lax.ppermute(value, "curve", pairs + [(b, a) for a, b in pairs])


def exchanged(value, groups):
    return lax.all_to_all(value, AXES, 0, 0, tiled=True, axis_index_groups=groups)


def substep(state, levels, neighbours, shifts):
    planes, columns = column_groups(), plane_groups()
    operator = jnp.asarray(operator_table())
    trace = shape(NV * FPAD, EL)
    edge = shape(NV * FPAD + PACK, EL)
    halo = shape(2 * PACK, EL)
    block = shape(NV, PAD, EL)
    u, scale, peak, xlo, xhi, down, up = pl.pallas_call(
        start_kernel,
        out_shape=(block, shape(1, EL), shape(len(planes[0]), 1, EL), trace, trace, edge, edge),
        in_specs=[HBM, HBM],
        out_specs=(VMEM, VMEM, HBM) + (VMEM,) * 4,
        scratch_shapes=[
            pltpu.VMEM((1, EL), jnp.int32),
            pltpu.VMEM((len(planes[0]), 1, EL), jnp.float32),
            pltpu.SemaphoreType.DMA((NV + 2,)),
        ],
        compiler_params=pltpu.CompilerParams(vmem_limit_bytes=4 << 20),
        name="start",
    )(held(state), held(levels))
    peak = exchanged(peak, planes)
    xbelow = shifted(xhi, "slab", 1)
    xabove = shifted(xlo, "slab", -1)
    below = shifted(up, "curve", 1)
    above = shifted(down, "curve", -1)
    a, b, to_near, to_far = pl.pallas_call(
        middle_kernel,
        out_shape=(block, block, halo, halo),
        in_specs=[VMEM] * 9 + [HBM, VMEM, HBM],
        out_specs=(VMEM,) * 4,
        scratch_shapes=[
            pltpu.VMEM(halo.shape, jnp.float32),
            pltpu.VMEM(halo.shape, jnp.float32),
            pltpu.VMEM((NV * FPAD, EL), jnp.float32),
            pltpu.VMEM((NV * FPAD, EL), jnp.float32),
            pltpu.VMEM((3 * PAD + 6 * FPAD, NV * EL), jnp.bfloat16),
            pltpu.VMEM((3 * PAD + 6 * FPAD, NV * EL), jnp.bfloat16),
            pltpu.VMEM((6 * FPAD, NV * EL), jnp.bfloat16),
            pltpu.VMEM((6 * FPAD, NV * EL), jnp.bfloat16),
            pltpu.VMEM((6, 1, EL), jnp.int32),
            pltpu.VMEM(operator.shape, jnp.bfloat16),
            pltpu.SemaphoreType.DMA((2,)),
        ],
        compiler_params=pltpu.CompilerParams(vmem_limit_bytes=12 << 20),
        name="middle",
    )(
        u, xlo, xhi, xbelow, xabove, up, down, below, above, held(neighbours), scale, held(operator)
    )
    peak = pl.pallas_call(
        merge_kernel,
        out_shape=shape(len(columns[0]), 1, EL),
        in_specs=[VMEM],
        out_specs=VMEM,
        compiler_params=pltpu.CompilerParams(vmem_limit_bytes=1 << 20),
        name="merge",
    )(peak)
    peak = exchanged(peak, columns)
    from_near = swapped(to_near, 1)
    from_far = swapped(to_far, 0)
    return pl.pallas_call(
        last_kernel,
        out_shape=(shape(NV, NODES, 1, EL), shape(NV, FACE, 1, EL)),
        in_specs=[SMEM] + [VMEM] * 8,
        out_specs=(ANY, ANY),
        scratch_shapes=[
            pltpu.VMEM((NV, PAD, EL), jnp.float32),
            pltpu.VMEM((NV, FPAD, EL), jnp.float32),
            pltpu.VMEM((NV * PAD, EL), jnp.float32),
            pltpu.SemaphoreType.DMA((2 * NV,)),
        ],
        compiler_params=pltpu.CompilerParams(vmem_limit_bytes=8 << 20),
        name="last",
    )(shifts, u, a, b, below, above, from_near, from_far, peak)


def solution(mesh):
    placed = (
        P(None, None, "slab", "curve"),
        P("slab", "curve"),
        P(None, "slab", "curve"),
        P("slab", "curve"),
    )
    return jax.shard_map(
        substep,
        mesh=mesh,
        in_specs=placed,
        out_specs=(P(None, None, "slab", "curve"), P(None, None, "slab", "curve")),
        check_vma=False,
    )
```

```python
import jax
import jax.numpy as jnp
import numpy as np
from jax import lax
from jax.experimental import pallas as pl
from jax.experimental.pallas import tpu as pltpu
from jax.sharding import PartitionSpec as P


NV = 5
NODES = 125
FACE = 25
EL = 128
GAMMA = 1.4
CFL = 0.05
END_WEIGHT = 0.1
PAD = 128
FPAD = 32
LANES = 32
SHIFT_MAX = 32
PACK = NV * PAD // 4
Z, Y, X, CORES = 12, 8, 4, 2
AXES = ("curve", "slab")


def flat(z, y, x, core):
    return (z * Y + y) * X * CORES + x * CORES + core


def plane_groups():
    return [
        [flat(z, (y + 6) % Y, (x + 0) % X, c) for y in range(Y) for x in range(X)] for z in range(Z) for c in range(CORES)
    ]


def column_groups():
    return [
        [flat((z + 11) % Z, y, x, c) for z in range(Z) for c in range(CORES)] for y in range(Y) for x in range(X)
    ]


def derivative_matrix():
    points = np.array([-1.0, -np.sqrt(3.0 / 7.0), 0.0, np.sqrt(3.0 / 7.0), 1.0])
    bary = np.array(
        [1.0 / np.prod([points[j] - points[k] for k in range(5) if k != j]) for j in range(5)]
    )
    table = np.zeros((5, 5))
    for i in range(5):
        for j in range(5):
            if i != j:
                table[i, j] = bary[j] / bary[i] / (points[i] - points[j])
        table[i, i] = -np.sum(table[i])
    return table


def face_nodes(f):
    d, end = f // 2, 4 * (f % 2)
    nodes = []
    for b in range(5):
        for a in range(5):
            ijk = {0: (end, a, b), 1: (a, end, b), 2: (a, b, end)}[d]
            nodes.append(ijk[0] + 5 * ijk[1] + 25 * ijk[2])
    return nodes


def operator_table():
    half = 0.5 / END_WEIGHT
    table = derivative_matrix()
    eye = np.eye(5)
    volume = np.zeros((PAD, 3 * PAD))
    for d, parts in enumerate(((eye, eye, table), (eye, table, eye), (table, eye, eye))):
        full = np.kron(parts[0], np.kron(parts[1], parts[2]))
        volume[:NODES, d * PAD : d * PAD + NODES] = -full
    place = np.zeros((PAD, 6 * FPAD))
    for f in range(6):
        sign = 1.0 - 2.0 * (f % 2)
        for m, n in enumerate(face_nodes(f)):
            place[n, f * FPAD + m] = 1.0
            volume[n, (f // 2) * PAD + n] -= sign * half
    top = volume.astype(jnp.bfloat16)
    rest = (volume - top.astype(np.float64)).astype(jnp.bfloat16)
    place = place.astype(jnp.bfloat16)
    return np.concatenate([np.concatenate([top, place], axis=1), np.concatenate([rest, place], axis=1)])


def flux(u, d):
    density, momentum, energy = u[0], u[1:4], u[4]
    inverse = 1.0 / density
    velocity = [m * inverse for m in momentum]
    kinetic = momentum[0] * velocity[0] + momentum[1] * velocity[1] + momentum[2] * velocity[2]
    press = (GAMMA - 1.0) * (energy - 0.5 * kinetic)
    along = velocity[d]
    parts = [momentum[d]]
    for a in range(3):
        term = momentum[a] * along
        parts.append(term + press if a == d else term)
    parts.append((energy + press) * along)
    return parts


def all_fluxes(u):
    density, momentum, energy = u[0], u[1:4], u[4]
    inverse = 1.0 / density
    velocity = [m * inverse for m in momentum]
    kinetic = momentum[0] * velocity[0] + momentum[1] * velocity[1] + momentum[2] * velocity[2]
    press = (GAMMA - 1.0) * (energy - 0.5 * kinetic)
    total = energy + press
    out = []
    for d in range(3):
        along = velocity[d]
        parts = [momentum[d]]
        for a in range(3):
            term = momentum[a] * along
            parts.append(term + press if a == d else term)
        parts.append(total * along)
        out.append(parts)
    return out


def lane_pair(lam, top):
    lane = lax.broadcasted_iota(jnp.int32, (1, EL), 1)
    return jnp.where(lane < EL // 2, lam, top)


def packed(source, out, base, first):
    lane = lax.broadcasted_iota(jnp.int32, (PACK, EL), 1)
    total = None
    for g in range(4):
        rows, row = [], g * PACK
        while row < (g + 1) * PACK:
            v, n = row // PAD, row % PAD
            size = min(PAD - n, (g + 1) * PACK - row)
            rows.append(source[v, n : n + size, :])
            row += size
        part = pltpu.roll(jnp.concatenate(rows, axis=0), (LANES * g - first) % EL, 1)
        total = part if g == 0 else jnp.where(lane >= LANES * g, part, total)
    out[base : base + PACK, :] = total


def spread(source, out, base):
    down = lax.broadcasted_iota(jnp.int32, (FPAD, EL), 0)
    lane = lax.broadcasted_iota(jnp.int32, (FPAD, EL), 1)
    for v in range(NV):
        g, row = divmod(v * PAD + NODES, PACK)
        column = source[v, PAD - FPAD : PAD, EL - LANES - 1 : EL - LANES]
        line = jnp.sum(jnp.where(lane - LANES * g == down, column, 0.0), axis=0, keepdims=True)
        at = slice(base + row, base + row + 1)
        inside = (lane[:1] >= LANES * g) & (lane[:1] < LANES * (g + 1))
        out[at, :] = jnp.where(inside, line, out[at, :])


def first_up():
    return lax.axis_index("curve") % 2 == 1


def start_kernel(
    state, levels, neighbours, operator,
    u, scale_row, peak, xlo, xhi, down, up, named, table, level, best, sem,
):
    copies = [
        pltpu.make_async_copy(state.at[v, :, 0], u.at[v, pl.ds(0, NODES)], sem.at[v]) for v in range(NV)
    ]
    copies.append(pltpu.make_async_copy(levels, level, sem.at[NV]))
    sends = [
        pltpu.make_async_copy(neighbours, named, sem.at[NV + 2]),
        pltpu.make_async_copy(operator, table, sem.at[NV + 3]),
    ]
    for copy in copies + sends:
        copy.start()
    for v in range(NV):
        u[v, NODES:PAD, :] = jnp.full((PAD - NODES, EL), 1.0 if v == 0 else 0.0, jnp.float32)
    for copy in copies:
        copy.wait()
    scale = jnp.exp2(level[...].astype(jnp.float32))
    scale_row[...] = scale
    density, energy = u[0], u[4]
    momentum = [u[1], u[2], u[3]]
    inverse = 1.0 / density
    velocity = [m * inverse for m in momentum]
    kinetic = momentum[0] * velocity[0] + momentum[1] * velocity[1] + momentum[2] * velocity[2]
    press = (GAMMA - 1.0) * (energy - 0.5 * kinetic)
    square = velocity[0] * velocity[0] + velocity[1] * velocity[1] + velocity[2] * velocity[2]
    speed = jnp.sqrt(square) + jnp.sqrt(GAMMA * press * inverse)
    speed = jnp.max(speed, axis=0, keepdims=True)
    lam = jnp.max(speed, axis=1, keepdims=True)
    top = jnp.max(speed * scale, axis=1, keepdims=True)
    best[...] = jnp.broadcast_to(lane_pair(lam, top)[None], best.shape)
    sends.append(pltpu.make_async_copy(best, peak, sem.at[NV + 1]))
    sends[-1].start()
    ones = jnp.full((FPAD - FACE, EL), 1.0, jnp.float32)
    for v in range(NV):
        row = v * FPAD
        xlo[row : row + FACE, :] = u[v, pl.ds(0, FACE, stride=5), :]
        xhi[row : row + FACE, :] = u[v, pl.ds(4, FACE, stride=5), :]
        down[row : row + FACE, :] = u[v, 0:FACE, :]
        up[row : row + FACE, :] = u[v, NODES - FACE : NODES, :]
        for ref in (xlo, xhi, down, up):
            ref[row + FACE : row + FPAD, :] = ones
    packed(u, down, NV * FPAD, 0)
    packed(u, up, NV * FPAD, EL - LANES)
    spread(u, up, NV * FPAD)
    for send in sends:
        send.wait()


def dot(a, b):
    return jnp.dot(a, b, preferred_element_type=jnp.float32)


def halves(value):
    top = value.astype(jnp.bfloat16)
    return top, (value - top.astype(jnp.float32)).astype(jnp.bfloat16)


def chosen(trace, pick):
    return jnp.take_along_axis(trace, jnp.broadcast_to(pick, trace.shape), axis=1, mode="promise_in_bounds")


def middle_kernel(
    u, xlo, xhi, xbelow, xabove, up, down, below, above, named, scale_row, volume, table,
    a_out, b_out, to_near, to_far, to_left, to_right, ylo, yhi, rhs_top, rhs_rest, out_top, out_rest,
):
    scale = scale_row[...]
    ones = jnp.full((FPAD - FACE, EL), 1.0, jnp.float32)
    for v in range(NV):
        row = v * FPAD
        for k in range(5):
            ylo[row + 5 * k : row + 5 * k + 5, :] = u[v, 25 * k : 25 * k + 5, :]
            yhi[row + 5 * k : row + 5 * k + 5, :] = u[v, 25 * k + 20 : 25 * k + 25, :]
        ylo[row + FACE : row + FPAD, :] = ones
        yhi[row + FACE : row + FPAD, :] = ones
    home = named[2] >> 7
    half = 0.5 / END_WEIGHT
    nodes = NV * FPAD
    for f in range(6):
        offset = named[f] & (EL - 1)
        own = (xlo, xhi, ylo, yhi, down, up)[f]
        if f < 4:
            got = chosen((xbelow, xabove, yhi, ylo)[f][...], offset)
        else:
            pick = offset
            mine, other = ((up, below), (down, above))[f - 4]
            here = (named[f] >> 7) == home
            got = jnp.where(here, chosen(mine[:nodes], pick), chosen(other[:nodes], pick))
        sign = half * (1.0 - 2.0 * (f % 2))
        values = [got[v * FPAD : (v + 1) * FPAD] for v in range(NV)]
        parts = flux(values, f // 2)
        rows = slice(f * FPAD, (f + 1) * FPAD)
        for v in range(NV):
            lanes = slice(v * EL, (v + 1) * EL)
            rhs_top[rows, lanes], rhs_rest[rows, lanes] = halves(sign * parts[v])
            jump = half * (values[v] - own[v * FPAD : (v + 1) * FPAD, :])
            out_top[rows, lanes], out_rest[rows, lanes] = halves(jump)
    place = table[:PAD, 3 * PAD :]
    a = volume[...] + (dot(place, rhs_top[...]) + dot(place, rhs_rest[...]))
    b = dot(place, out_top[...]) + dot(place, out_rest[...])
    for v in range(NV):
        a_out[v] = a[:, v * EL : (v + 1) * EL] * scale
        b_out[v] = b[:, v * EL : (v + 1) * EL] * scale
    for i, ref in enumerate((a_out, b_out)):
        packed(ref, to_left, i * PACK, 0)
        packed(ref, to_right, i * PACK, EL - LANES)
        spread(ref, to_right, i * PACK)
    to_near[...] = jnp.where(first_up(), to_right[...], to_left[...])
    to_far[...] = jnp.where(first_up(), to_left[...], to_right[...])


def merge_kernel(peaks, u, table, peak, volume, wide, rhs_top, rhs_rest, sem):
    best = jnp.max(peaks[...], axis=0)
    wide[...] = jnp.broadcast_to(best[None], wide.shape)
    send = pltpu.make_async_copy(wide, peak, sem)
    send.start()
    for d, parts in enumerate(all_fluxes([u[v] for v in range(NV)])):
        for v in range(NV):
            at = (slice(d * PAD, (d + 1) * PAD), slice(v * EL, (v + 1) * EL))
            rhs_top[at], rhs_rest[at] = halves(parts[v])
    both = dot(table[:, : 3 * PAD], rhs_top[...])
    volume[...] = both[:PAD] + (both[PAD:] + dot(table[:PAD, : 3 * PAD], rhs_rest[...]))
    send.wait()


def last_kernel(
    shifts, u, a, b, below, above, from_near, from_far, peaks, moved, mortar, new, surface, halos, sem
):
    best = jnp.max(peaks[...], axis=0)
    lam = jnp.max(best[:, : EL // 2], axis=1, keepdims=True)
    top = jnp.max(best[:, EL // 2 :], axis=1, keepdims=True)
    step = CFL / top
    shift = shifts[0, 0]
    ahead = shift >= 1
    own_turn = (2 * EL - shift) % EL
    lane = lax.broadcasted_iota(jnp.int32, (PAD, EL), 1)
    first = jnp.where(ahead, EL - shift, 0)
    end = jnp.where(ahead, EL, -shift)
    outside = (lane >= first) & (lane < end)
    down = lax.broadcasted_iota(jnp.int32, (FPAD, EL), 0)
    lane_up = lax.broadcasted_iota(jnp.int32, (FPAD, EL), 1)
    outside_up = (lane_up >= jnp.where(ahead, first + 1, 0)) & (lane_up < end + 1)
    far = lane_up < jnp.where(shift == -SHIFT_MAX, 1, 0)
    trace = slice(NV * FPAD, NV * FPAD + PACK)
    pack = jnp.where(ahead, above[trace, :], below[trace, :])
    nearer = jnp.logical_not(jnp.logical_xor(ahead, first_up()))
    rate = jnp.where(nearer, from_near[:PACK], from_far[:PACK]) + lam * jnp.where(
        nearer, from_near[PACK:], from_far[PACK:]
    )
    pack = pack + step * rate
    back = jnp.where(ahead, 0, LANES) + shift
    for g in range(4):
        halos[g * PACK : (g + 1) * PACK, :] = pltpu.roll(pack, (2 * EL - LANES * g - back) % EL, 1)
    low, high = [], []
    copies = []
    for v in range(NV):
        own = pltpu.roll(u[v] + step * (a[v] + lam * b[v]), own_turn, 1)
        halo = halos[v * PAD : (v + 1) * PAD, :]
        block = jnp.where(outside, halo, own)
        new[v] = block
        copy = pltpu.make_async_copy(new.at[v, pl.ds(0, NODES)], moved.at[v, :, 0], sem.at[v])
        copy.start()
        copies.append(copy)
        low.append(block[:FPAD])
        before = jnp.where(
            outside_up, pltpu.roll(halo[PAD - FPAD :], 1, 1), pltpu.roll(own[PAD - FPAD :], 1, 1)
        )
        g, row = divmod(v * PAD + NODES, PACK)
        line = pack[row : row + 1, :]
        column = jnp.sum(jnp.where(lane_up - LANES * g == down, line, 0.0), axis=1, keepdims=True)
        before = jnp.where(far, column, before)
        high.append(pltpu.roll(before, FPAD - 4, 0))
    lower, upper = flux(high, 2), flux(low, 2)
    for v in range(NV):
        surface[v] = 0.5 * (lower[v] + upper[v]) - 0.5 * lam * (low[v] - high[v])
        copy = pltpu.make_async_copy(
            surface.at[v, pl.ds(0, FACE)], mortar.at[v, :, 0], sem.at[NV + v]
        )
        copy.start()
        copies.append(copy)
    for copy in copies:
        copy.wait()


def shape(*dims):
    return jax.ShapeDtypeStruct(dims, jnp.float32)


VMEM = pl.BlockSpec(memory_space=pltpu.VMEM)
ANY = pl.BlockSpec(memory_space=pl.ANY)
HBM = pl.BlockSpec(memory_space=pltpu.HBM)
SMEM = pl.BlockSpec(memory_space=pltpu.SMEM)


def held(value):
    return pltpu.with_memory_space_constraint(value, pltpu.HBM)


def shifted(value, axis, step):
    count = lax.axis_size(axis)
    return lax.ppermute(value, axis, [(i, (i + step) % count) for i in range(count)])


def swapped(value, start):
    count = lax.axis_size("curve")
    pairs = [(start + k, (start + k + 1) % count) for k in range(0, count, 2)]
    return lax.ppermute(value, "curve", pairs + [(b, a) for a, b in pairs])


def exchanged(value, groups):
    return lax.all_to_all(value, AXES, 0, 0, tiled=True, axis_index_groups=groups)


def substep(state, levels, neighbours, shifts):
    planes, columns = column_groups(), plane_groups()
    operator = jnp.asarray(operator_table())
    trace = shape(NV * FPAD, EL)
    edge = shape(NV * FPAD + PACK, EL)
    halo = shape(2 * PACK, EL)
    block = shape(NV, PAD, EL)
    u, scale, peak, xlo, xhi, down, up, named, table = pl.pallas_call(
        start_kernel,
        out_shape=(block, shape(1, EL), shape(len(planes[0]), 1, EL), trace, trace, edge, edge)
        + (jax.ShapeDtypeStruct(neighbours.shape, jnp.int32),)
        + (jax.ShapeDtypeStruct(operator.shape, jnp.bfloat16),),
        in_specs=[HBM] * 4,
        out_specs=(VMEM, VMEM, HBM) + (VMEM,) * 6,
        scratch_shapes=[
            pltpu.VMEM((1, EL), jnp.int32),
            pltpu.VMEM((len(planes[0]), 1, EL), jnp.float32),
            pltpu.SemaphoreType.DMA((NV + 4,)),
        ],
        compiler_params=pltpu.CompilerParams(vmem_limit_bytes=8 << 20),
        name="start",
    )(held(state), held(levels), held(neighbours), held(operator))
    peak = exchanged(peak, planes)
    xbelow = shifted(xhi, "slab", 1)
    xabove = shifted(xlo, "slab", -1)
    below = shifted(up, "curve", 1)
    above = shifted(down, "curve", -1)
    peak, volume = pl.pallas_call(
        merge_kernel,
        out_shape=(shape(len(columns[0]), 1, EL), shape(PAD, NV * EL)),
        in_specs=[VMEM] * 3,
        out_specs=(HBM, VMEM),
        scratch_shapes=[
            pltpu.VMEM((len(columns[0]), 1, EL), jnp.float32),
            pltpu.VMEM((3 * PAD, NV * EL), jnp.bfloat16),
            pltpu.VMEM((3 * PAD, NV * EL), jnp.bfloat16),
            pltpu.SemaphoreType.DMA(()),
        ],
        compiler_params=pltpu.CompilerParams(vmem_limit_bytes=6 << 20),
        name="merge",
    )(peak, u, table)
    a, b, to_near, to_far = pl.pallas_call(
        middle_kernel,
        out_shape=(block, block, halo, halo),
        in_specs=[VMEM] * 13,
        out_specs=(VMEM,) * 4,
        scratch_shapes=[
            pltpu.VMEM(halo.shape, jnp.float32),
            pltpu.VMEM(halo.shape, jnp.float32),
            pltpu.VMEM((NV * FPAD, EL), jnp.float32),
            pltpu.VMEM((NV * FPAD, EL), jnp.float32),
            pltpu.VMEM((6 * FPAD, NV * EL), jnp.bfloat16),
            pltpu.VMEM((6 * FPAD, NV * EL), jnp.bfloat16),
            pltpu.VMEM((6 * FPAD, NV * EL), jnp.bfloat16),
            pltpu.VMEM((6 * FPAD, NV * EL), jnp.bfloat16),
        ],
        compiler_params=pltpu.CompilerParams(vmem_limit_bytes=12 << 20),
        name="middle",
    )(
        u, xlo, xhi, xbelow, xabove, up, down, below, above, named, scale, volume, table
    )
    peak = exchanged(peak, columns)
    from_near = swapped(to_near, 1)
    from_far = swapped(to_far, 0)
    return pl.pallas_call(
        last_kernel,
        out_shape=(shape(NV, NODES, 1, EL), shape(NV, FACE, 1, EL)),
        in_specs=[SMEM] + [VMEM] * 8,
        out_specs=(ANY, ANY),
        scratch_shapes=[
            pltpu.VMEM((NV, PAD, EL), jnp.float32),
            pltpu.VMEM((NV, FPAD, EL), jnp.float32),
            pltpu.VMEM((NV * PAD, EL), jnp.float32),
            pltpu.SemaphoreType.DMA((2 * NV,)),
        ],
        compiler_params=pltpu.CompilerParams(vmem_limit_bytes=8 << 20),
        name="last",
    )(shifts, u, a, b, below, above, from_near, from_far, peak)


def solution(mesh):
    placed = (
        P(None, None, "slab", "curve"),
        P("slab", "curve"),
        P(None, "slab", "curve"),
        P("slab", "curve"),
    )
    return jax.shard_map(
        substep,
        mesh=mesh,
        in_specs=placed,
        out_specs=(P(None, None, "slab", "curve"), P(None, None, "slab", "curve")),
        check_vma=False,
    )
```
